32 devices in a mesh: groups: 2 (over x), inst: 8 (over z, y), tp: 2 (over core).
Axes of the slice: x: 2, y: 2, z: 4, core: 2. Of those that a mesh axis runs over, the one named last changes fastest.
Arguments:
- queries: bfloat16 [4, 512, 3072], P(None, ('groups', 'inst'), 'tp'), parts along dimension 1, may hold values from -130 to 130
- new_kv: bfloat16 [4, 512, 256], P(None, ('groups', 'inst')), parts along dimension 1, may hold values from -4.5 to 4.5
- cache_pool: bfloat16 [98304, 256], P(('groups', 'inst')), parts along dimension 0, may hold values from -6 to 6
- lengths: int32 [16, 32], P('groups'), parts along dimension 0, may hold values from 1 to 2, as said below
- anchor: int32 [16, 32], P('groups'), parts along dimension 0, may hold values from 0 to 7, as said below
- out_weight: bfloat16 [3072, 3072], P('tp'), may hold values from -0.875 to 0.875
Outputs:
- attended: bfloat16 [4, 512, 3072], P(None, ('groups', 'inst'), 'tp'), parts along dimension 1
The draws below stay inside these ranges and needn't reach their ends.
There are 2 independent parts, one for each index of `groups`. The reference program is written for one: setup_inputs(seed, part) draws one part's arguments, and reference() takes and returns one part's arrays. A program takes and returns all parts, laid end to end along the dimension named above; an argument that names none is the same for every part. Nothing has to cross between parts.
Inputs may be any that keep to these rules, and one draw needn't show every extreme that they name: `lengths`: in every instance exactly 16 requests hold 2 blocks and the others one; the requests' blocks lie in the instance's pool in slot order, each right after the one before, filling its 48 blocks. anchor[d, j] is the instance whose request in slot j moves to slot j of instance d, or d where the slot stays. Exactly 7 slots move; for each of them the source is the destination rotated by one amount, nonzero and different for each moving slot, and one of these amounts is half the number of instances, rounded down; so every instance sends and receives exactly 7 requests, at most one to or from any other instance.
All inputs are finite; a program needn't handle non-finite values.
Results may differ from the reference program's by a relative error of at most 0.009.
Values may be sent and summed in bfloat16 or wider, within the bound.
A program may use at most 128 MiB of HBM per device.

```python
import math
import jax
import jax.numpy as jnp
from jax import lax

D = 3072
HEADS = 24
HDIM = 128
BLK = 128
MAXB = 2
STEPS = 4
R = 32
KVW = 256
CAPB = 48
MIG = 7
N_INST = 8


def plan_parts(key):
    base = jax.random.fold_in(key, 7)
    key_slots, key_shift, key_len = jax.random.split(base, 3)
    order = jax.random.permutation(key_slots, R).astype(jnp.int32)
    half_turn = N_INST // 2
    others = (jax.random.permutation(key_shift, N_INST - 2) + 1).astype(jnp.int32)
    others = others + (others >= half_turn).astype(jnp.int32)
    rotations = jnp.concatenate([jnp.full((1,), half_turn, jnp.int32), others])
    moving = order[:MIG]
    shift_slot = jnp.zeros((R,), jnp.int32).at[moving].set(rotations[:MIG])
    dest_index = jnp.arange(N_INST, dtype=jnp.int32)
    anchor = (dest_index[:, None] - shift_slot[None, :]) % N_INST
    row_keys = jax.random.split(key_len, N_INST)
    ranks = jax.vmap(lambda row_key: jax.random.permutation(row_key, R))(row_keys)
    lengths = 1 + (ranks < R // 2).astype(jnp.int32)
    return (anchor.astype(jnp.int32), lengths.astype(jnp.int32))


def draw_lengths(key, part):
    return plan_parts(key)[1]


def draw_anchor(key, part):
    return plan_parts(key)[0]


def token_parts(key):
    base = jax.random.fold_in(key, 11)
    key_query, key_keys, key_values = jax.random.split(base, 3)
    total_rows = N_INST * R
    keys_new = jax.random.truncated_normal(key_keys, -4.5, 4.5, (STEPS, total_rows, HDIM), jnp.float32)
    values_new = jax.random.truncated_normal(key_values, -4.5, 4.5, (STEPS, total_rows, HDIM), jnp.float32)
    noise = jax.random.truncated_normal(key_query, -4.5, 4.5, (STEPS, total_rows, HEADS, HDIM), jnp.float32)
    queries = noise + 0.27 * keys_new[:, :, None, :]
    return (queries.reshape(STEPS, total_rows, HEADS * HDIM), jnp.concatenate([keys_new, values_new], axis=-1))


def draw_queries(key, part):
    return token_parts(key)[0].astype(jnp.bfloat16)


def draw_new_kv(key, part):
    return token_parts(key)[1].astype(jnp.bfloat16)


def shard_levels(own_key, dims, cuts, low, largest):
    def one(position, parts):
        draws = jax.random.uniform(jax.random.fold_in(jax.random.fold_in(own_key, 6), position), (parts,), jnp.float32, low / len(cuts), largest / len(cuts))
        return jnp.repeat(jnp.exp(draws), dims[position] // parts).reshape((-1,) + (1,) * (len(dims) - position - 1))

    level = one(*cuts[0])
    for cut in cuts[1:]:
        level = level * one(*cut)
    return level


def bell_draw(own_key, extent, spread, most, shards=(), held_as=jnp.bfloat16):
    loudness = shard_levels(own_key, extent, shards, -0.22, 0.18) if shards else 1.0
    entries = jax.random.normal(own_key, extent, jnp.float32) * spread * loudness
    return jnp.minimum(jnp.maximum(entries, -most), most).astype(held_as)


def setup_inputs(seed: int = 0, part: int = 0) -> dict:
    arg_keys = jax.random.split(jax.random.key(seed), 7)
    own_keys = jax.random.split(jax.random.fold_in(arg_keys[6], part), 7)
    return {
        "queries": draw_queries(jax.random.fold_in(jax.random.fold_in(arg_keys[6], part), 71), part),
        "new_kv": draw_new_kv(jax.random.fold_in(jax.random.fold_in(arg_keys[6], part), 71), part),
        "cache_pool": bell_draw(own_keys[2], (N_INST * CAPB * BLK, KVW), 1.0, 6.0, ((0, 8),)),
        "lengths": draw_lengths(jax.random.fold_in(jax.random.fold_in(arg_keys[6], part), 71), part),
        "anchor": draw_anchor(jax.random.fold_in(jax.random.fold_in(arg_keys[6], part), 71), part),
        "out_weight": bell_draw(arg_keys[5], (HEADS * HDIM, D), (HEADS * HDIM // 64) ** -0.5, 0.875, ((0, 2),)),
    }


def reference(queries, new_kv, cache_pool, lengths, anchor, out_weight):
    window_rows = MAXB * BLK
    pool_rows = CAPB * BLK
    slot_ids = jnp.arange(R, dtype=jnp.int32)
    within = jnp.arange(window_rows, dtype=jnp.int32)
    step_ids = jnp.arange(STEPS, dtype=jnp.int32)
    offsets = (jnp.cumsum(lengths, axis=1) - lengths).astype(jnp.int32)
    score_scale = 1.0 / math.sqrt(HDIM)
    causal = step_ids[:, None] >= step_ids[None, :]

    def per_instance(dest):
        source = anchor[dest]
        start_row = (source * pool_rows + offsets[source, slot_ids] * BLK).astype(jnp.int32)
        row_count = lengths[source, slot_ids] * BLK
        row_index = jnp.minimum(start_row[:, None] + within[None, :], cache_pool.shape[0] - 1)
        cached = cache_pool[row_index]
        valid_rows = within[None, :] < row_count[:, None]
        query_part = lax.dynamic_slice_in_dim(queries, (dest * R).astype(jnp.int32), R, 1)
        fresh_rows = lax.dynamic_slice_in_dim(new_kv, (dest * R).astype(jnp.int32), R, 1)
        query_heads = query_part.astype(jnp.float32).reshape(STEPS, R, HEADS, HDIM)
        cache_keys = cached[:, :, :HDIM].astype(jnp.float32)
        cache_values = cached[:, :, HDIM:].astype(jnp.float32)
        fresh_keys = fresh_rows[:, :, :HDIM].astype(jnp.float32)
        fresh_values = fresh_rows[:, :, HDIM:].astype(jnp.float32)
        cache_scores = jnp.einsum('srhe,rte->srht', query_heads, cache_keys) * score_scale
        cache_scores = jnp.where(valid_rows[None, :, None, :], cache_scores, -jnp.inf)
        fresh_scores = jnp.einsum('srhe,ure->srhu', query_heads, fresh_keys) * score_scale
        fresh_scores = jnp.where(causal[:, None, None, :], fresh_scores, -jnp.inf)
        row_max = jnp.maximum(lax.optimization_barrier(jnp.max(cache_scores, axis=-1)), lax.optimization_barrier(jnp.max(fresh_scores, axis=-1)))
        exp_cache = jnp.exp(cache_scores - row_max[..., None])
        exp_fresh = jnp.exp(fresh_scores - row_max[..., None])
        denominator = lax.optimization_barrier(jnp.sum(exp_cache, axis=-1)) + lax.optimization_barrier(jnp.sum(exp_fresh, axis=-1))
        weight_cache = (exp_cache / denominator[..., None]).astype(jnp.bfloat16).astype(jnp.float32)
        weight_fresh = (exp_fresh / denominator[..., None]).astype(jnp.bfloat16).astype(jnp.float32)
        head_out = jnp.einsum('srht,rte->srhe', weight_cache, cache_values)
        head_out = head_out + jnp.einsum('srhu,ure->srhe', weight_fresh, fresh_values)
        attn = head_out.reshape(STEPS * R, HEADS * HDIM).astype(jnp.bfloat16)
        projected = jnp.dot(attn, out_weight, preferred_element_type=jnp.float32)
        return projected.reshape(STEPS, R, D).astype(jnp.bfloat16)
    per_dest = lax.map(per_instance, jnp.arange(N_INST, dtype=jnp.int32))
    return jnp.transpose(per_dest, (1, 0, 2, 3)).reshape(STEPS, N_INST * R, D)
```

```python
import functools
import math

import jax
import jax.numpy as jnp
from jax import lax
from jax.experimental import pallas as pl
from jax.experimental.pallas import tpu as pltpu
from jax.sharding import PartitionSpec as P

HDIM = 128
BLK = 128
MAXB = 2
MESH = pl.DeviceIdType.MESH
EDGE = 1
MAIN_FIRST = 2
NT = (((1,), (1,)), ((), ()))


def grouped(count, unroll, fn):
    full = count // unroll
    if full == 1:
        fn([i for i in range(unroll)])
    elif full > 1:

        def step(g, carry):
            fn([g * unroll + u for u in range(unroll)])
            return carry

        lax.fori_loop(0, full, step, 0)
    rest = list(range(full * unroll, count))
    if rest:
        fn(rest)


def kernel(
    n, edge, cols, q_hbm, kv_hbm, pool_hbm, len_hbm, anc_hbm, w_hbm, out_ref,
    q_in, kv_in, pool, w_buf, item, res, fin, lhs, causal,
    q_out, q_got, r_out, r_got, o_out, o_got, m_out, m_got, main, own, back, moved_lhs, spread,
    push_out, push_got,
    len_s, anc_s, shift_s, off_s, stay_s, nxt_s, slot_s, used_s, free_s, pos_s,
    in_sem, w_sem, q_send, q_recv, r_send, r_recv, x_send, o_recv, m_recv, p_sem,
):
    steps, slots, width = q_in.shape
    heads = width // HDIM
    rows = steps * heads
    span = rows + 2 * steps
    window = MAXB * BLK
    blocks = pool_hbm.shape[0]
    half = out_ref.shape[2]
    chunks = half // cols
    peers = n - 1
    stays = slots - peers
    me = lax.axis_index("inst")
    tp = lax.axis_index("tp")
    crowded = peers <= slots // 4
    mirror = n - 1 - me
    is_early = me < edge
    is_late = mirror < edge
    push_k = 2 * jnp.minimum(me, mirror)

    copy_len = pltpu.make_async_copy(len_hbm, len_s, in_sem.at[0])
    copy_anc = pltpu.make_async_copy(anc_hbm, anc_s, in_sem.at[1])
    copy_q = pltpu.make_async_copy(q_hbm, q_in, in_sem.at[2])
    copy_kv = pltpu.make_async_copy(kv_hbm, kv_in, in_sem.at[3])
    copy_pool = pltpu.make_async_copy(pool_hbm, pool.at[pl.ds(0, blocks)], in_sem.at[4])
    copy_len.start()
    copy_anc.start()
    copy_q.start()
    copy_kv.start()
    copy_pool.start()
    copy_w = []
    for c in range(2 * chunks):
        side = (1 - tp) if c < chunks else tp
        column = pl.multiple_of(side * half + (c % chunks) * cols, cols)
        copy_w.append(
            pltpu.make_async_copy(w_hbm.at[:, pl.ds(column, cols)], w_buf.at[c], w_sem.at[c])
        )

    def peer(k):
        return {"inst": lax.rem(me + k, n)}

    barrier = pltpu.get_barrier_semaphore()
    for k in range(peers):

        @pl.when(jnp.logical_not(is_late & (push_k == k)))
        def _():
            pl.semaphore_signal(barrier, inc=1, device_id=peer(k + 1), device_id_type=MESH)

    pl.semaphore_signal(barrier, inc=1, device_id={"tp": 1 - tp}, device_id_type=MESH)

    def scan_slot(j, carry):
        off, found = carry
        turn = me - anc_s[me, j]
        turn = jnp.where(turn < 0, turn + n, turn)
        shift_s[j] = turn
        off_s[j] = off
        found = tuple(jnp.where(turn == k + 1, j, found[k]) for k in range(peers))
        return off + len_s[me, j], found

    copy_len.wait()
    copy_anc.wait()
    _, found = lax.fori_loop(
        0, slots, scan_slot, (jnp.int32(0), tuple(jnp.int32(-1) for _ in range(peers))),
        unroll=8,
    )

    flat = item.reshape(slots * span, HDIM)
    copy_q.wait()
    copy_kv.wait()
    for t in range(steps):
        for h in range(heads):
            flat[pl.ds(t * heads + h, slots, stride=span), :] = q_in[
                t, :, h * HDIM : (h + 1) * HDIM
            ].astype(jnp.float32)
        for part in range(2):
            flat[pl.ds(rows + part * steps + t, slots, stride=span), :] = kv_in[
                t, :, part * HDIM : (part + 1) * HDIM
            ].astype(jnp.float32)

    def item_of(slot):
        return item[slot]

    for k in range(peers):
        q_out[k] = item_of(jnp.maximum(found[k], 0)).astype(jnp.bfloat16)

    def send_q(k):
        return pltpu.make_async_remote_copy(
            src_ref=q_out.at[k], dst_ref=q_got.at[k], send_sem=q_send,
            recv_sem=q_recv, device_id=peer(n - 1 - k), device_id_type=MESH,
        )

    def send_r(k):
        return pltpu.make_async_remote_copy(
            src_ref=r_out.at[k], dst_ref=r_got.at[k], send_sem=r_send,
            recv_sem=r_recv, device_id=peer(k + 1), device_id_type=MESH,
        )

    def send_o(c):
        return pltpu.make_async_remote_copy(
            src_ref=o_out.at[c], dst_ref=o_got.at[c], send_sem=x_send.at[0],
            recv_sem=o_recv, device_id={"tp": 1 - tp}, device_id_type=MESH,
        )

    def send_m(c):
        return pltpu.make_async_remote_copy(
            src_ref=m_out.at[c], dst_ref=m_got.at[c], send_sem=x_send.at[1],
            recv_sem=m_recv.at[c], device_id={"tp": 1 - tp}, device_id_type=MESH,
        )

    push = pltpu.make_async_remote_copy(
        src_ref=push_out, dst_ref=push_got.at[tp], send_sem=p_sem.at[0],
        recv_sem=p_sem.at[1], device_id={"inst": mirror}, device_id_type=MESH,
    )
    relay = pltpu.make_async_remote_copy(
        src_ref=push_got.at[tp], dst_ref=push_got.at[tp], send_sem=p_sem.at[0],
        recv_sem=p_sem.at[2], device_id={"tp": 1 - tp}, device_id_type=MESH,
    )

    group = 5
    full = stays // group

    def all_but_one(fewer, ref, sem):
        @pl.when(fewer)
        def _():
            if peers > 1:
                part = ref.at[pl.ds(0, peers - 1)]
                pltpu.make_async_copy(part, part, sem).wait()

        @pl.when(jnp.logical_not(fewer))
        def _():
            pltpu.make_async_copy(ref, ref, sem).wait()

    def meet():
        pl.semaphore_wait(barrier, jnp.where(is_early, n - 1, n))
        for k in range(peers):

            @pl.when(jnp.logical_not(is_early & (push_k == k)))
            def _():
                send_q(k).start()

    meet_at = jnp.where(me == 0, full, jnp.clip((mirror - 1) // 2 * 2 - 1, 0, full))

    for k in range(peers):
        slot_s[k] = jnp.maximum(found[k], 0)
    push_slot = slot_s[push_k]

    def scan_next(i, cur):
        j = slots - 1 - i
        cur = jnp.where(shift_s[j] == 0, j, cur)
        nxt_s[j] = cur
        return cur

    lax.fori_loop(0, slots, scan_next, jnp.int32(slots - 1), unroll=True)

    def scan_stay(i, cur):
        stay_s[i] = cur
        return nxt_s[jnp.minimum(cur + 1, slots - 1)]

    lax.fori_loop(0, slots, scan_stay, nxt_s[0], unroll=True)
    spare = jnp.int32(0)
    for k in range(peers):
        slot_s[k] = jnp.where(found[k] >= 0, found[k], stay_s[stays + spare])
        used_s[k] = jnp.where(found[k] >= 0, 1, 0)
        spare = spare + jnp.where(found[k] >= 0, 0, 1)
    nxt = jnp.int32(peers - 1)
    for k in reversed(range(peers)):
        nxt = jnp.where(found[k] >= 0, nxt, k)
        nxt_s[k] = nxt
    nxt = nxt_s[0]
    for k in range(peers):
        free_s[k] = nxt
        nxt = nxt_s[jnp.minimum(nxt + 1, peers - 1)]

    def scan_pos(j, count):
        turn = shift_s[j]
        extra = free_s[jnp.clip(count - stays, 0, peers - 1)]
        rest = jnp.where(count < stays, count, stays + extra)
        pos_s[j] = jnp.where(turn > 0, stays + turn - 1, rest)
        return count + jnp.where(turn > 0, 0, 1)

    lax.fori_loop(0, slots, scan_pos, jnp.int32(0), unroll=True)

    pool[blocks] = jnp.zeros((BLK, 2 * HDIM), pool.dtype)
    row_id = lax.broadcasted_iota(jnp.int32, (rows, 2 * steps), 0)
    col_id = lax.broadcasted_iota(jnp.int32, (rows, 2 * steps), 1)
    causal[...] = jnp.where((col_id < steps) & (row_id >= col_id * heads), 0.0, -jnp.inf)

    factor = math.log2(math.e) / math.sqrt(HDIM)
    key_id = lax.broadcasted_iota(jnp.int32, (1, window), 1)

    def cached(j):
        return jnp.concatenate([pool[off_s[j] + b] for b in range(MAXB)], axis=0)

    def attend(items, caches, lens):
        added = [x[rows:] for x in items]
        new_keys = [x.astype(jnp.bfloat16) for x in added]
        new_values = [pltpu.roll(x, steps, 0).astype(jnp.bfloat16) for x in added]
        items = [x[:rows].astype(jnp.bfloat16) for x in items]
        scores, fresh = [], []
        for x, y, cache, size in zip(items, new_keys, caches, lens):
            s = lax.dot_general(
                x, cache()[:, :HDIM], NT, preferred_element_type=jnp.float32
            )
            scores.append(jnp.where(key_id < size * BLK, s, -jnp.inf))
            s = lax.dot_general(x, y, NT, preferred_element_type=jnp.float32)
            fresh.append(s + causal[...])
        tops = [
            jnp.maximum(jnp.max(s, axis=1, keepdims=True), jnp.max(f, axis=1, keepdims=True))
            for s, f in zip(scores, fresh)
        ]
        scores = [jnp.exp2((s - m) * factor) for s, m in zip(scores, tops)]
        fresh = [jnp.exp2((f - m) * factor) for f, m in zip(fresh, tops)]
        results = []
        for y, s, f, cache in zip(new_values, scores, fresh, caches):
            total = jnp.sum(s, axis=1, keepdims=True) + jnp.sum(f, axis=1, keepdims=True)
            o = jnp.dot(
                s.astype(jnp.bfloat16), cache()[:, HDIM:],
                preferred_element_type=jnp.float32,
            )
            o = o + jnp.dot(
                f.astype(jnp.bfloat16), y, preferred_element_type=jnp.float32
            )
            results.append(o / total)
        return results

    def attend_own(items, owners):
        return attend(
            items,
            [functools.partial(cached, j) for j in owners],
            [len_s[me, j] for j in owners],
        )

    def put(i, value):
        res[i] = value

    def stay_group(indices):
        owners = [stay_s[i] for i in indices]
        for i, o in zip(indices, attend_own([item_of(j) for j in owners], owners)):
            put(i, o)

    def move_group(ks):
        owners = [slot_s[k] for k in ks]
        sent = [(used_s[k] > 0) & jnp.logical_not(is_late & (push_k == k)) for k in ks]
        items = [
            jnp.where(ok, q_got[k].astype(jnp.float32), item_of(j))
            for k, j, ok in zip(ks, owners, sent)
        ]
        for k, o in zip(ks, attend_own(items, owners)):
            put(stays + k, o)
            r_out[k] = o.astype(jnp.bfloat16)
        for k in ks:

            @pl.when(jnp.logical_not(is_late & (push_k == k)))
            def _():
                send_r(k).start()

    pl.when(meet_at == 0)(meet)
    copy_pool.wait()
    for copy in copy_w:
        copy.start()

    @pl.when(is_late)
    def _():
        push_out[...] = pool[off_s[push_slot] + tp]
        push.start()

    def stay_step(g, carry):
        stay_group([g * group + u for u in range(group)])

        pl.when(meet_at == g + 1)(meet)
        return carry

    lax.fori_loop(0, full, stay_step, 0)
    if stays > full * group:
        stay_group(list(range(full * group, stays)))

    def serve():
        all_but_one(is_late, q_got, q_recv)
        grouped(peers, 7, move_group)

    if not crowded:
        serve()

    def gather(j, carry):
        own_rows = res[pos_s[j]]
        fin[pl.ds(pl.multiple_of(j * rows, 8), rows), :] = jnp.where(
            shift_s[j] > 0, jnp.zeros_like(own_rows), own_rows
        )
        return carry

    lax.fori_loop(0, slots, gather, 0, unroll=8)
    for t in range(steps):
        for h in range(heads):
            lhs[t * slots : (t + 1) * slots, h * HDIM : (h + 1) * HDIM] = fin[
                pl.ds(t * heads + h, slots, stride=rows), :
            ].astype(jnp.bfloat16)
    for c in range(chunks):
        copy_w[c].wait()
        o_out[c] = jnp.dot(lhs[...], w_buf[c], preferred_element_type=jnp.float32).astype(
            jnp.bfloat16
        )
        send_o(c).start()

    if crowded:
        pl.when(me >= MAIN_FIRST)(serve)
    for c in range(chunks):
        copy_w[chunks + c].wait()
        main[c] = jnp.dot(lhs[...], w_buf[chunks + c], preferred_element_type=jnp.float32)

    pad = back.shape[0]
    row_id = lax.broadcasted_iota(jnp.int32, (slots, steps * pad), 0)
    col_id = lax.broadcasted_iota(jnp.int32, (slots, steps * pad), 1)
    turns = jnp.zeros((slots, steps * pad), jnp.int32)
    for j in range(slots):
        turns = jnp.where(row_id == j, shift_s[j], turns)
    for t in range(steps):
        spread[t * slots : (t + 1) * slots, :] = jnp.where(
            (turns > 0) & (col_id == turns + (t * pad - 1)), 1.0, 0.0
        ).astype(jnp.bfloat16)

    @pl.when(is_early)
    def _():
        push.wait_recv()
        relay.start()

    if crowded:
        pl.when(me < MAIN_FIRST)(serve)

    @pl.when(is_early)
    def _():
        relay.wait_recv()
        (o,) = attend(
            [item_of(push_slot)],
            [lambda: jnp.concatenate([push_got[b] for b in range(MAXB)], axis=0)],
            [len_s[mirror, push_slot]],
        )
        r_got[push_k] = o.astype(jnp.bfloat16)

    all_but_one(is_early, r_got, r_recv)
    for k in range(peers, pad):
        back[k] = jnp.zeros((rows, HDIM), jnp.float32)
    for k in range(peers):
        back[k] = r_got[k].astype(jnp.float32)
    flat_back = back.reshape(pad * rows, HDIM)
    for t in range(steps):
        for h in range(heads):
            moved_lhs[t * pad : (t + 1) * pad, h * HDIM : (h + 1) * HDIM] = flat_back[
                pl.ds(t * heads + h, pad, stride=rows), :
            ]
    moved = moved_lhs[...].astype(jnp.bfloat16)
    for c in range(chunks):
        m_out[c] = jnp.dot(moved, w_buf[c], preferred_element_type=jnp.float32).astype(
            jnp.bfloat16
        )
        send_m(c).start()
    pltpu.make_async_copy(o_got, o_got, o_recv).wait()
    for c in range(chunks):
        own[c] = jnp.dot(moved, w_buf[chunks + c], preferred_element_type=jnp.float32)
        main[c] = main[c] + o_got[c].astype(jnp.float32)
    for c in range(chunks):
        send_m(c).wait_recv()
        total = (own[c] + m_got[c].astype(jnp.float32)).astype(jnp.bfloat16)
        total = jnp.dot(spread[...], total, preferred_element_type=jnp.float32)
        total = (total + main[c]).astype(out_ref.dtype)
        for t in range(steps):
            out_ref[t, :, c * cols : (c + 1) * cols] = total[t * slots : (t + 1) * slots]
    all_but_one(is_early, q_out, q_send)
    all_but_one(is_late, r_out, r_send)
    pltpu.make_async_copy(o_out, o_out, x_send.at[0]).wait()
    pltpu.make_async_copy(m_out, m_out, x_send.at[1]).wait()

    @pl.when(is_late)
    def _():
        push.wait_send()

    @pl.when(is_early)
    def _():
        relay.wait_send()


def body(n, queries, new_kv, cache_pool, lengths, anchor, out_weight):
    steps, slots, width = queries.shape
    features = out_weight.shape[1]
    half = features // lax.axis_size("tp")
    cols = 768 if half % 768 == 0 else half
    chunks = half // cols
    rows = steps * (width // HDIM)
    span = rows + 2 * steps
    peers = n - 1
    pad = -(-peers // 8) * 8
    blocks = cache_pool.shape[0] // BLK
    edge = min(EDGE, n // 4)
    bf16, f32, i32 = jnp.bfloat16, jnp.float32, jnp.int32
    dma = pltpu.SemaphoreType.DMA
    anywhere = pl.BlockSpec(memory_space=pltpu.HBM)
    cache = cache_pool.reshape(blocks, BLK, 2 * HDIM)
    queries, new_kv, cache, lengths, anchor, out_weight = (
        pltpu.with_memory_space_constraint(x, pltpu.HBM)
        for x in (queries, new_kv, cache, lengths, anchor, out_weight)
    )
    return pl.pallas_call(
        functools.partial(kernel, n, edge, cols),
        out_shape=jax.ShapeDtypeStruct((steps, slots, half), bf16),
        in_specs=[anywhere] * 6,
        out_specs=pl.BlockSpec(memory_space=pltpu.VMEM),
        scratch_shapes=[
            pltpu.VMEM(queries.shape, bf16),
            pltpu.VMEM(new_kv.shape, bf16),
            pltpu.VMEM((blocks + MAXB - 1, BLK, 2 * HDIM), bf16),
            pltpu.VMEM((2 * chunks, width, cols), bf16),
            pltpu.VMEM((slots, span, HDIM), f32),
            pltpu.VMEM((slots, rows, HDIM), f32),
            pltpu.VMEM((slots * rows, HDIM), f32),
            pltpu.VMEM((steps * slots, width), bf16),
            pltpu.VMEM((rows, 2 * steps), f32),
            pltpu.VMEM((peers, span, HDIM), bf16),
            pltpu.VMEM((peers, span, HDIM), bf16),
            pltpu.VMEM((peers, rows, HDIM), bf16),
            pltpu.VMEM((peers, rows, HDIM), bf16),
            pltpu.VMEM((chunks, steps * slots, cols), bf16),
            pltpu.VMEM((chunks, steps * slots, cols), bf16),
            pltpu.VMEM((chunks, steps * pad, cols), bf16),
            pltpu.VMEM((chunks, steps * pad, cols), bf16),
            pltpu.VMEM((chunks, steps * slots, cols), f32),
            pltpu.VMEM((chunks, steps * pad, cols), f32),
            pltpu.VMEM((pad, rows, HDIM), f32),
            pltpu.VMEM((steps * pad, width), f32),
            pltpu.VMEM((steps * slots, steps * pad), bf16),
            pltpu.VMEM((BLK, 2 * HDIM), bf16),
            pltpu.VMEM((MAXB, BLK, 2 * HDIM), bf16),
        ]
        + [pltpu.SMEM(lengths.shape, i32), pltpu.SMEM(anchor.shape, i32)]
        + [pltpu.SMEM((max(slots, n),), i32)] * 8
        + [dma((5,)), dma((2 * chunks,))]
        + [dma(())] * 4
        + [dma((2,)), dma(()), dma((chunks,)), dma((3,))],
        compiler_params=pltpu.CompilerParams(
            collective_id=0, has_side_effects=True, vmem_limit_bytes=48 * 1024 * 1024
        ),
    )(queries, new_kv, cache, lengths, anchor, out_weight)


def solution(mesh):
    n = mesh.shape["inst"]
    placed = (
        P(None, ("groups", "inst"), "tp"),
        P(None, ("groups", "inst"), None),
        P(("groups", "inst"), None),
        P("groups", None),
        P("groups", None),
        P("tp", None),
    )
    return jax.shard_map(
        functools.partial(body, n),
        mesh=mesh,
        in_specs=placed,
        out_specs=P(None, ("groups", "inst"), "tp"),
        check_vma=False,
    )
```

```python
import functools
import math

import jax
import jax.numpy as jnp
from jax import lax
from jax.experimental import pallas as pl
from jax.experimental.pallas import tpu as pltpu
from jax.sharding import PartitionSpec as P

HDIM = 128
BLK = 128
MAXB = 2
MESH = pl.DeviceIdType.MESH
NT = (((1,), (1,)), ((), ()))


def grouped(count, unroll, fn):
    full = count // unroll
    if full == 1:
        fn([i for i in range(unroll)])
    elif full > 1:

        def step(g, carry):
            fn([g * unroll + u for u in range(unroll)])
            return carry

        lax.fori_loop(0, full, step, 0)
    rest = list(range(full * unroll, count))
    if rest:
        fn(rest)


def kernel(
    n, edge, cols, q_hbm, kv_hbm, pool_hbm, len_hbm, anc_hbm, w_hbm, out_ref,
    q_in, kv_in, pool, w_buf, item, res, fin, lhs, causal,
    q_out, q_got, r_out, r_got, o_out, o_got, m_out, m_got, main, own, back, moved_lhs, spread,
    push_out, push_got,
    len_s, anc_s, shift_s, off_s, stay_s, nxt_s, slot_s, used_s, free_s, pos_s,
    in_sem, w_sem, q_send, q_recv, r_send, r_recv, x_send, o_recv, m_recv, p_sem,
):
    steps, slots, width = q_in.shape
    heads = width // HDIM
    rows = steps * heads
    span = rows + 2 * steps
    window = MAXB * BLK
    blocks = pool_hbm.shape[0]
    half = out_ref.shape[2]
    chunks = half // cols
    peers = n - 1
    stays = slots - peers
    me = lax.axis_index("inst")
    tp = lax.axis_index("tp")
    crowded = peers <= slots // 4
    mirror = n - 1 - me
    is_early = me < edge
    is_late = mirror < edge
    push_k = 0
    band = n // 2
    upper = lax.div(me, band)
    place = lax.rem(me, band)
    deepest = lax.div(lax.rem(me + n - 1, n) + 2, n)

    copy_len = pltpu.make_async_copy(len_hbm, len_s, in_sem.at[0])
    copy_anc = pltpu.make_async_copy(anc_hbm, anc_s, in_sem.at[1])
    copy_q = pltpu.make_async_copy(q_hbm, q_in, in_sem.at[2])
    copy_kv = pltpu.make_async_copy(kv_hbm, kv_in, in_sem.at[3])
    copy_pool = pltpu.make_async_copy(pool_hbm, pool.at[pl.ds(0, blocks)], in_sem.at[4])
    copy_len.start()
    copy_anc.start()
    copy_q.start()
    copy_kv.start()
    copy_pool.start()
    copy_w = []
    for c in range(2 * chunks):
        side = (1 - tp) if c < chunks else tp
        column = pl.multiple_of(side * half + (c % chunks) * cols, cols)
        copy_w.append(
            pltpu.make_async_copy(w_hbm.at[:, pl.ds(column, cols)], w_buf.at[c], w_sem.at[c])
        )

    def peer(k):
        return {"inst": lax.rem(me + k, n)}

    barrier = pltpu.get_barrier_semaphore()
    for k in range(peers):

        @pl.when(jnp.logical_not(is_late & (push_k == k)))
        def _():
            pl.semaphore_signal(barrier, inc=1, device_id=peer(k + 1), device_id_type=MESH)

    pl.semaphore_signal(barrier, inc=1, device_id={"tp": 1 - tp}, device_id_type=MESH)

    def scan_slot(j, carry):
        off, found = carry
        turn = me - anc_s[me, j]
        turn = jnp.where(turn < 0, turn + n, turn)
        shift_s[j] = turn
        off_s[j] = off
        found = tuple(jnp.where(turn == k + 1, j, found[k]) for k in range(peers))
        return off + len_s[me, j], found

    copy_len.wait()
    copy_anc.wait()
    _, found = lax.fori_loop(
        0, slots, scan_slot, (jnp.int32(0), tuple(jnp.int32(-1) for _ in range(peers))),
        unroll=8,
    )

    flat = item.reshape(slots * span, HDIM)
    copy_q.wait()
    copy_kv.wait()
    for t in range(steps):
        for h in range(heads):
            flat[pl.ds(t * heads + h, slots, stride=span), :] = q_in[
                t, :, h * HDIM : (h + 1) * HDIM
            ].astype(jnp.float32)
        for part in range(2):
            flat[pl.ds(rows + part * steps + t, slots, stride=span), :] = kv_in[
                t, :, part * HDIM : (part + 1) * HDIM
            ].astype(jnp.float32)

    def item_of(slot):
        return item[slot]

    for k in range(peers):
        q_out[k] = item_of(jnp.maximum(found[k], 0)).astype(jnp.bfloat16)

    def batch_to(k):
        across = lax.rem(lax.div(lax.rem(me + n - 1 - k, n), band) + upper, 2)
        return across * (1 + deepest)

    def send_q(k):
        return pltpu.make_async_remote_copy(
            src_ref=q_out.at[k], dst_ref=q_got.at[k], send_sem=q_send,
            recv_sem=q_recv.at[batch_to(k)], device_id=peer(n - 1 - k), device_id_type=MESH,
        )

    def send_r(k):
        return pltpu.make_async_remote_copy(
            src_ref=r_out.at[k], dst_ref=r_got.at[k], send_sem=r_send,
            recv_sem=r_recv, device_id=peer(k + 1), device_id_type=MESH,
        )

    def send_o(c):
        return pltpu.make_async_remote_copy(
            src_ref=o_out.at[c], dst_ref=o_got.at[c], send_sem=x_send.at[0],
            recv_sem=o_recv, device_id={"tp": 1 - tp}, device_id_type=MESH,
        )

    def send_m(c):
        return pltpu.make_async_remote_copy(
            src_ref=m_out.at[c], dst_ref=m_got.at[c], send_sem=x_send.at[1],
            recv_sem=m_recv.at[c], device_id={"tp": 1 - tp}, device_id_type=MESH,
        )

    push = pltpu.make_async_remote_copy(
        src_ref=push_out, dst_ref=push_got.at[tp], send_sem=p_sem.at[0],
        recv_sem=p_sem.at[1], device_id={"inst": mirror}, device_id_type=MESH,
    )
    relay = pltpu.make_async_remote_copy(
        src_ref=push_got.at[tp], dst_ref=push_got.at[tp], send_sem=p_sem.at[0],
        recv_sem=p_sem.at[2], device_id={"tp": 1 - tp}, device_id_type=MESH,
    )

    group = 5
    full = stays // group

    def all_but_one(fewer, ref, sem):
        @pl.when(fewer)
        def _():
            if peers > 1:
                part = ref.at[pl.ds(0, peers - 1)]
                pltpu.make_async_copy(part, part, sem).wait()

        @pl.when(jnp.logical_not(fewer))
        def _():
            pltpu.make_async_copy(ref, ref, sem).wait()

    def greet():
        pl.semaphore_wait(barrier, jnp.where(is_early, n - 1, n))

    def send_all_q():
        for k in range(peers):

            @pl.when(jnp.logical_not(is_early & (push_k == k)))
            def _():
                send_q(k).start()

    def meet():
        greet()
        send_all_q()

    meet_at = jnp.where(me == 0, full, jnp.clip((mirror - 1) // 2 * 2 - 1, 0, full))

    for k in range(peers):
        slot_s[k] = jnp.maximum(found[k], 0)
    push_slot = slot_s[push_k]

    def scan_next(i, cur):
        j = slots - 1 - i
        cur = jnp.where(shift_s[j] == 0, j, cur)
        nxt_s[j] = cur
        return cur

    lax.fori_loop(0, slots, scan_next, jnp.int32(slots - 1), unroll=True)

    def scan_stay(i, cur):
        stay_s[i] = cur
        return nxt_s[jnp.minimum(cur + 1, slots - 1)]

    lax.fori_loop(0, slots, scan_stay, nxt_s[0], unroll=True)
    spare = jnp.int32(0)
    for k in range(peers):
        slot_s[k] = jnp.where(found[k] >= 0, found[k], stay_s[stays + spare])
        used_s[k] = jnp.where(found[k] >= 0, 1, 0)
        spare = spare + jnp.where(found[k] >= 0, 0, 1)
    nxt = jnp.int32(peers - 1)
    for k in reversed(range(peers)):
        nxt = jnp.where(found[k] >= 0, nxt, k)
        nxt_s[k] = nxt
    nxt = nxt_s[0]
    for k in range(peers):
        free_s[k] = nxt
        nxt = nxt_s[jnp.minimum(nxt + 1, peers - 1)]

    def scan_pos(j, count):
        turn = shift_s[j]
        extra = free_s[jnp.clip(count - stays, 0, peers - 1)]
        rest = jnp.where(count < stays, count, stays + extra)
        pos_s[j] = jnp.where(turn > 0, stays + turn - 1, rest)
        return count + jnp.where(turn > 0, 0, 1)

    lax.fori_loop(0, slots, scan_pos, jnp.int32(0), unroll=True)

    pool[blocks] = jnp.zeros((BLK, 2 * HDIM), pool.dtype)
    row_id = lax.broadcasted_iota(jnp.int32, (rows, 2 * steps), 0)
    col_id = lax.broadcasted_iota(jnp.int32, (rows, 2 * steps), 1)
    causal[...] = jnp.where((col_id < steps) & (row_id >= col_id * heads), 0.0, -jnp.inf)

    factor = math.log2(math.e) / math.sqrt(HDIM)
    key_id = lax.broadcasted_iota(jnp.int32, (1, window), 1)

    def cached(j):
        return jnp.concatenate([pool[off_s[j] + b] for b in range(MAXB)], axis=0)

    def attend(items, caches, lens):
        added = [x[rows:] for x in items]
        new_keys = [x.astype(jnp.bfloat16) for x in added]
        new_values = [pltpu.roll(x, steps, 0).astype(jnp.bfloat16) for x in added]
        items = [x[:rows].astype(jnp.bfloat16) for x in items]
        scores, fresh = [], []
        for x, y, cache, size in zip(items, new_keys, caches, lens):
            s = lax.dot_general(
                x, cache()[:, :HDIM], NT, preferred_element_type=jnp.float32
            )
            scores.append(jnp.where(key_id < size * BLK, s, -jnp.inf))
            s = lax.dot_general(x, y, NT, preferred_element_type=jnp.float32)
            fresh.append(s + causal[...])
        tops = [
            jnp.maximum(jnp.max(s, axis=1, keepdims=True), jnp.max(f, axis=1, keepdims=True))
            for s, f in zip(scores, fresh)
        ]
        scores = [jnp.exp2((s - m) * factor) for s, m in zip(scores, tops)]
        fresh = [jnp.exp2((f - m) * factor) for f, m in zip(fresh, tops)]
        results = []
        for y, s, f, cache in zip(new_values, scores, fresh, caches):
            total = jnp.sum(s, axis=1, keepdims=True) + jnp.sum(f, axis=1, keepdims=True)
            o = jnp.dot(
                s.astype(jnp.bfloat16), cache()[:, HDIM:],
                preferred_element_type=jnp.float32,
            )
            o = o + jnp.dot(
                f.astype(jnp.bfloat16), y, preferred_element_type=jnp.float32
            )
            results.append(o / total)
        return results

    def attend_own(items, owners):
        return attend(
            items,
            [functools.partial(cached, j) for j in owners],
            [len_s[me, j] for j in owners],
        )

    def put(i, value):
        res[i] = value

    def stay_group(indices):
        owners = [stay_s[i] for i in indices]
        for i, o in zip(indices, attend_own([item_of(j) for j in owners], owners)):
            put(i, o)

    def move_group(ks):
        owners = [slot_s[k] for k in ks]
        sent = [(used_s[k] > 0) & jnp.logical_not(is_late & (push_k == k)) for k in ks]
        items = [
            jnp.where(ok, q_got[k].astype(jnp.float32), item_of(j))
            for k, j, ok in zip(ks, owners, sent)
        ]
        for k, o in zip(ks, attend_own(items, owners)):
            put(stays + k, o)
            r_out[k] = o.astype(jnp.bfloat16)
        for i in range(len(ks)):
            k = upper * ks[len(ks) - 1 - i] + (1 - upper) * ks[i]

            @pl.when(jnp.logical_not(is_late & (push_k == k)))
            def _():
                send_r(k).start()

    pl.when(meet_at == 0)(meet)
    copy_pool.wait()
    for copy in copy_w:
        copy.start()

    @pl.when(is_late)
    def _():
        push_out[...] = pool[off_s[push_slot] + tp]
        push.start()

    def stay_step(g, carry):
        stay_group([g * group + u for u in range(group)])

        pl.when(meet_at == g + 1)(meet)
        return carry

    lax.fori_loop(0, full, stay_step, 0)
    if stays > full * group:
        stay_group(list(range(full * group, stays)))

    def arrived(count, batch):
        if count > 0:
            got = q_got.at[pl.ds(0, count)]
            pltpu.make_async_copy(got, got, q_recv.at[batch]).wait()

    def serve_near():
        arrived(band - 1, 0)

        def rotation(i):
            other = i + lax.div(i + band - place, band)
            return lax.rem(other - place - 1 + n, n)

        grouped(band - 1, 7, lambda idx: move_group([rotation(i) for i in idx]))

    def far_rotation(i):
        owner = upper * (band - 1 - i) + (1 - upper) * (band + i)
        return lax.rem(owner - me - 1 + n, n)

    def serve_shallow():
        arrived(band - 1, 1)
        grouped(band - 1, 7, lambda idx: move_group([far_rotation(i) for i in idx]))

    def serve_deep():
        pl.when(jnp.logical_not(is_late))(lambda: arrived(1, 2))
        move_group([far_rotation(band - 1)])

    def serve(step):
        if crowded and step == 1:

            @pl.when(upper > 0)
            def _():
                pl.when(jnp.logical_not(is_late))(serve_deep)
                serve_near()
                serve_shallow()

            @pl.when((upper == 0) & jnp.logical_not(is_early))
            def _():
                serve_near()
                serve_shallow()

        elif crowded and step == 2:

            @pl.when(is_early)
            def _():
                serve_near()
                serve_shallow()

            pl.when(upper == 0)(serve_deep)
        elif not crowded and step == 0:
            serve_near()
            serve_shallow()
            serve_deep()

    serve(0)

    def gather(j, carry):
        own_rows = res[pos_s[j]]
        fin[pl.ds(pl.multiple_of(j * rows, 8), rows), :] = jnp.where(
            shift_s[j] > 0, jnp.zeros_like(own_rows), own_rows
        )
        return carry

    lax.fori_loop(0, slots, gather, 0, unroll=8)
    for t in range(steps):
        for h in range(heads):
            lhs[t * slots : (t + 1) * slots, h * HDIM : (h + 1) * HDIM] = fin[
                pl.ds(t * heads + h, slots, stride=rows), :
            ].astype(jnp.bfloat16)
    for c in range(chunks):
        copy_w[c].wait()
        o_out[c] = jnp.dot(lhs[...], w_buf[c], preferred_element_type=jnp.float32).astype(
            jnp.bfloat16
        )
        send_o(c).start()

    serve(1)
    for c in range(chunks):
        copy_w[chunks + c].wait()
        main[c] = jnp.dot(lhs[...], w_buf[chunks + c], preferred_element_type=jnp.float32)

    pad = back.shape[0]
    row_id = lax.broadcasted_iota(jnp.int32, (slots, steps * pad), 0)
    col_id = lax.broadcasted_iota(jnp.int32, (slots, steps * pad), 1)
    turns = jnp.zeros((slots, steps * pad), jnp.int32)
    for j in range(slots):
        turns = jnp.where(row_id == j, shift_s[j], turns)
    for t in range(steps):
        spread[t * slots : (t + 1) * slots, :] = jnp.where(
            (turns > 0) & (col_id == turns + (t * pad - 1)), 1.0, 0.0
        ).astype(jnp.bfloat16)

    serve(2)

    @pl.when(is_early)
    def _():
        push.wait_recv()
        relay.start()

    @pl.when(is_early)
    def _():
        relay.wait_recv()
        (o,) = attend(
            [item_of(push_slot)],
            [lambda: jnp.concatenate([push_got[b] for b in range(MAXB)], axis=0)],
            [len_s[mirror, push_slot]],
        )
        r_got[push_k] = o.astype(jnp.bfloat16)

    all_but_one(is_early, r_got, r_recv)
    for k in range(peers, pad):
        back[k] = jnp.zeros((rows, HDIM), jnp.float32)
    for k in range(peers):
        back[k] = r_got[k].astype(jnp.float32)
    flat_back = back.reshape(pad * rows, HDIM)
    for t in range(steps):
        for h in range(heads):
            moved_lhs[t * pad : (t + 1) * pad, h * HDIM : (h + 1) * HDIM] = flat_back[
                pl.ds(t * heads + h, pad, stride=rows), :
            ]
    moved = moved_lhs[...].astype(jnp.bfloat16)
    for c in range(chunks):
        m_out[c] = jnp.dot(moved, w_buf[c], preferred_element_type=jnp.float32).astype(
            jnp.bfloat16
        )
        send_m(c).start()
    pltpu.make_async_copy(o_got, o_got, o_recv).wait()
    for c in range(chunks):
        own[c] = jnp.dot(moved, w_buf[chunks + c], preferred_element_type=jnp.float32)
        main[c] = main[c] + o_got[c].astype(jnp.float32)
    for c in range(chunks):
        send_m(c).wait_recv()
        total = (own[c] + m_got[c].astype(jnp.float32)).astype(jnp.bfloat16)
        total = jnp.dot(spread[...], total, preferred_element_type=jnp.float32)
        total = (total + main[c]).astype(out_ref.dtype)
        for t in range(steps):
            out_ref[t, :, c * cols : (c + 1) * cols] = total[t * slots : (t + 1) * slots]
    all_but_one(is_early, q_out, q_send)
    all_but_one(is_late, r_out, r_send)
    pltpu.make_async_copy(o_out, o_out, x_send.at[0]).wait()
    pltpu.make_async_copy(m_out, m_out, x_send.at[1]).wait()

    @pl.when(is_late)
    def _():
        push.wait_send()

    @pl.when(is_early)
    def _():
        relay.wait_send()


def body(n, queries, new_kv, cache_pool, lengths, anchor, out_weight):
    steps, slots, width = queries.shape
    features = out_weight.shape[1]
    half = features // lax.axis_size("tp")
    cols = 768 if half % 768 == 0 else half
    chunks = half // cols
    rows = steps * (width // HDIM)
    span = rows + 2 * steps
    peers = n - 1
    pad = -(-peers // 8) * 8
    blocks = cache_pool.shape[0] // BLK
    edge = min(1, n // 4)
    bf16, f32, i32 = jnp.bfloat16, jnp.float32, jnp.int32
    dma = pltpu.SemaphoreType.DMA
    anywhere = pl.BlockSpec(memory_space=pltpu.HBM)
    cache = cache_pool.reshape(blocks, BLK, 2 * HDIM)
    queries, new_kv, cache, lengths, anchor, out_weight = (
        pltpu.with_memory_space_constraint(x, pltpu.HBM)
        for x in (queries, new_kv, cache, lengths, anchor, out_weight)
    )
    return pl.pallas_call(
        functools.partial(kernel, n, edge, cols),
        out_shape=jax.ShapeDtypeStruct((steps, slots, half), bf16),
        in_specs=[anywhere] * 6,
        out_specs=pl.BlockSpec(memory_space=pltpu.VMEM),
        scratch_shapes=[
            pltpu.VMEM(queries.shape, bf16),
            pltpu.VMEM(new_kv.shape, bf16),
            pltpu.VMEM((blocks + MAXB - 1, BLK, 2 * HDIM), bf16),
            pltpu.VMEM((2 * chunks, width, cols), bf16),
            pltpu.VMEM((slots, span, HDIM), f32),
            pltpu.VMEM((slots, rows, HDIM), f32),
            pltpu.VMEM((slots * rows, HDIM), f32),
            pltpu.VMEM((steps * slots, width), bf16),
            pltpu.VMEM((rows, 2 * steps), f32),
            pltpu.VMEM((peers, span, HDIM), bf16),
            pltpu.VMEM((peers, span, HDIM), bf16),
            pltpu.VMEM((peers, rows, HDIM), bf16),
            pltpu.VMEM((peers, rows, HDIM), bf16),
            pltpu.VMEM((chunks, steps * slots, cols), bf16),
            pltpu.VMEM((chunks, steps * slots, cols), bf16),
            pltpu.VMEM((chunks, steps * pad, cols), bf16),
            pltpu.VMEM((chunks, steps * pad, cols), bf16),
            pltpu.VMEM((chunks, steps * slots, cols), f32),
            pltpu.VMEM((chunks, steps * pad, cols), f32),
            pltpu.VMEM((pad, rows, HDIM), f32),
            pltpu.VMEM((steps * pad, width), f32),
            pltpu.VMEM((steps * slots, steps * pad), bf16),
            pltpu.VMEM((BLK, 2 * HDIM), bf16),
            pltpu.VMEM((MAXB, BLK, 2 * HDIM), bf16),
        ]
        + [pltpu.SMEM(lengths.shape, i32), pltpu.SMEM(anchor.shape, i32)]
        + [pltpu.SMEM((max(slots, n),), i32)] * 8
        + [dma((5,)), dma((2 * chunks,))]
        + [dma(()), dma((3,)), dma(()), dma(())]
        + [dma((2,)), dma(()), dma((chunks,)), dma((3,))],
        compiler_params=pltpu.CompilerParams(
            collective_id=0, has_side_effects=True, vmem_limit_bytes=48 * 1024 * 1024
        ),
    )(queries, new_kv, cache, lengths, anchor, out_weight)


def solution(mesh):
    n = mesh.shape["inst"]
    placed = (
        P(None, ("groups", "inst"), "tp"),
        P(None, ("groups", "inst"), None),
        P(("groups", "inst"), None),
        P("groups", None),
        P("groups", None),
        P("tp", None),
    )
    return jax.shard_map(
        functools.partial(body, n),
        mesh=mesh,
        in_specs=placed,
        out_specs=P(None, ("groups", "inst"), "tp"),
        check_vma=False,
    )
```

```python
import functools
import math

import jax
import jax.numpy as jnp
from jax import lax
from jax.experimental import pallas as pl
from jax.experimental.pallas import tpu as pltpu
from jax.sharding import PartitionSpec as P

HDIM = 128
BLK = 128
MAXB = 2
MESH = pl.DeviceIdType.MESH
NT = (((1,), (1,)), ((), ()))


def grouped(count, unroll, fn):
    full = count // unroll
    if full == 1:
        fn([i for i in range(unroll)])
    elif full > 1:

        def step(g, carry):
            fn([g * unroll + u for u in range(unroll)])
            return carry

        lax.fori_loop(0, full, step, 0)
    rest = list(range(full * unroll, count))
    if rest:
        fn(rest)


def kernel(
    n, edge, cols, q_hbm, kv_hbm, pool_hbm, len_hbm, anc_hbm, w_hbm, out_ref,
    q_in, kv_in, pool, w_buf, item, res, fin, lhs, causal,
    q_out, q_got, r_out, r_got, o_out, o_got, m_out, m_got, main, own, back, moved_lhs, spread,
    push_out, push_got,
    len_s, anc_s, shift_s, off_s, stay_s, nxt_s, slot_s, used_s, free_s, pos_s,
    in_sem, w_sem, q_send, q_recv, r_send, r_recv, x_send, o_recv, m_recv, p_sem,
):
    steps, slots, width = q_in.shape
    heads = width // HDIM
    rows = steps * heads
    span = rows + 2 * steps
    window = MAXB * BLK
    blocks = pool_hbm.shape[0]
    half = out_ref.shape[2]
    chunks = half // cols
    peers = n - 1
    stays = slots - peers
    me = lax.axis_index("inst")
    tp = lax.axis_index("tp")
    crowded = peers <= slots // 4
    mirror = n - 1 - me
    is_early = me < edge
    is_late = mirror < edge
    push_k = 0
    band = n // 2
    upper = lax.div(me, band)
    place = lax.rem(me, band)
    deepest = lax.div(lax.rem(me + n - 1, n) + 2, n)

    copy_len = pltpu.make_async_copy(len_hbm, len_s, in_sem.at[0])
    copy_anc = pltpu.make_async_copy(anc_hbm, anc_s, in_sem.at[1])
    copy_q = pltpu.make_async_copy(q_hbm, q_in, in_sem.at[2])
    copy_kv = pltpu.make_async_copy(kv_hbm, kv_in, in_sem.at[3])
    copy_pool = pltpu.make_async_copy(pool_hbm, pool.at[pl.ds(0, blocks)], in_sem.at[4])
    copy_len.start()
    copy_anc.start()
    copy_q.start()
    copy_kv.start()
    copy_pool.start()
    copy_w = []
    for c in range(2 * chunks):
        side = (1 - tp) if c < chunks else tp
        column = pl.multiple_of(side * half + (c % chunks) * cols, cols)
        copy_w.append(
            pltpu.make_async_copy(w_hbm.at[:, pl.ds(column, cols)], w_buf.at[c], w_sem.at[c])
        )

    def peer(k):
        return {"inst": lax.rem(me + k, n)}

    barrier = pltpu.get_barrier_semaphore()
    for k in range(peers):

        @pl.when(jnp.logical_not(is_late & (push_k == k)))
        def _():
            pl.semaphore_signal(barrier, inc=1, device_id=peer(k + 1), device_id_type=MESH)

    pl.semaphore_signal(barrier, inc=1, device_id={"tp": 1 - tp}, device_id_type=MESH)

    def scan_slot(j, carry):
        off, found = carry
        turn = me - anc_s[me, j]
        turn = jnp.where(turn < 0, turn + n, turn)
        shift_s[j] = turn
        off_s[j] = off
        found = tuple(jnp.where(turn == k + 1, j, found[k]) for k in range(peers))
        return off + len_s[me, j], found

    copy_len.wait()
    copy_anc.wait()
    _, found = lax.fori_loop(
        0, slots, scan_slot, (jnp.int32(0), tuple(jnp.int32(-1) for _ in range(peers))),
        unroll=8,
    )

    flat = item.reshape(slots * span, HDIM)
    copy_q.wait()
    copy_kv.wait()
    for t in range(steps):
        for h in range(heads):
            flat[pl.ds(t * heads + h, slots, stride=span), :] = q_in[
                t, :, h * HDIM : (h + 1) * HDIM
            ].astype(jnp.float32)
        for part in range(2):
            flat[pl.ds(rows + part * steps + t, slots, stride=span), :] = kv_in[
                t, :, part * HDIM : (part + 1) * HDIM
            ].astype(jnp.float32)

    def item_of(slot):
        return item[slot]

    for k in range(peers):
        q_out[k] = item_of(jnp.maximum(found[k], 0)).astype(jnp.bfloat16)

    def batch_to(k):
        across = lax.rem(lax.div(lax.rem(me + n - 1 - k, n), band) + upper, 2)
        return across * (1 + deepest)

    def send_q(k):
        return pltpu.make_async_remote_copy(
            src_ref=q_out.at[k], dst_ref=q_got.at[k], send_sem=q_send,
            recv_sem=q_recv.at[batch_to(k)], device_id=peer(n - 1 - k), device_id_type=MESH,
        )

    def send_r(k):
        return pltpu.make_async_remote_copy(
            src_ref=r_out.at[k], dst_ref=r_got.at[k], send_sem=r_send,
            recv_sem=r_recv, device_id=peer(k + 1), device_id_type=MESH,
        )

    send_o = pltpu.make_async_remote_copy(
        src_ref=o_out, dst_ref=o_got, send_sem=x_send.at[0],
        recv_sem=o_recv, device_id={"tp": 1 - tp}, device_id_type=MESH,
    )
    send_m = pltpu.make_async_remote_copy(
        src_ref=m_out, dst_ref=m_got, send_sem=x_send.at[1],
        recv_sem=m_recv, device_id={"tp": 1 - tp}, device_id_type=MESH,
    )
    push = pltpu.make_async_remote_copy(
        src_ref=push_out, dst_ref=push_got.at[tp], send_sem=p_sem.at[0],
        recv_sem=p_sem.at[1], device_id={"inst": mirror}, device_id_type=MESH,
    )
    relay = pltpu.make_async_remote_copy(
        src_ref=push_got.at[tp], dst_ref=push_got.at[tp], send_sem=p_sem.at[0],
        recv_sem=p_sem.at[2], device_id={"tp": 1 - tp}, device_id_type=MESH,
    )

    group = 5
    full = stays // group

    def all_but_one(fewer, ref, sem):
        @pl.when(fewer)
        def _():
            if peers > 1:
                part = ref.at[pl.ds(0, peers - 1)]
                pltpu.make_async_copy(part, part, sem).wait()

        @pl.when(jnp.logical_not(fewer))
        def _():
            pltpu.make_async_copy(ref, ref, sem).wait()

    def greet():
        pl.semaphore_wait(barrier, jnp.where(is_early, n - 1, n))

    def send_all_q():
        for k in range(peers):

            @pl.when(jnp.logical_not(is_early & (push_k == k)))
            def _():
                send_q(k).start()

    def meet():
        greet()
        send_all_q()

    meet_at = jnp.where(me == 0, full, jnp.clip((mirror - 1) // 2 * 2 - 1, 0, full))

    for k in range(peers):
        slot_s[k] = jnp.maximum(found[k], 0)
    push_slot = slot_s[push_k]

    def scan_next(i, cur):
        j = slots - 1 - i
        cur = jnp.where(shift_s[j] == 0, j, cur)
        nxt_s[j] = cur
        return cur

    lax.fori_loop(0, slots, scan_next, jnp.int32(slots - 1), unroll=True)

    def scan_stay(i, cur):
        stay_s[i] = cur
        return nxt_s[jnp.minimum(cur + 1, slots - 1)]

    lax.fori_loop(0, slots, scan_stay, nxt_s[0], unroll=True)
    spare = jnp.int32(0)
    for k in range(peers):
        slot_s[k] = jnp.where(found[k] >= 0, found[k], stay_s[stays + spare])
        used_s[k] = jnp.where(found[k] >= 0, 1, 0)
        spare = spare + jnp.where(found[k] >= 0, 0, 1)
    nxt = jnp.int32(peers - 1)
    for k in reversed(range(peers)):
        nxt = jnp.where(found[k] >= 0, nxt, k)
        nxt_s[k] = nxt
    nxt = nxt_s[0]
    for k in range(peers):
        free_s[k] = nxt
        nxt = nxt_s[jnp.minimum(nxt + 1, peers - 1)]

    def scan_pos(j, count):
        turn = shift_s[j]
        extra = free_s[jnp.clip(count - stays, 0, peers - 1)]
        rest = jnp.where(count < stays, count, stays + extra)
        pos_s[j] = jnp.where(turn > 0, stays + turn - 1, rest)
        return count + jnp.where(turn > 0, 0, 1)

    lax.fori_loop(0, slots, scan_pos, jnp.int32(0), unroll=True)

    pool[blocks] = jnp.zeros((BLK, 2 * HDIM), pool.dtype)
    row_id = lax.broadcasted_iota(jnp.int32, (rows, 2 * steps), 0)
    col_id = lax.broadcasted_iota(jnp.int32, (rows, 2 * steps), 1)
    causal[...] = jnp.where((col_id < steps) & (row_id >= col_id * heads), 0.0, -jnp.inf)

    factor = math.log2(math.e) / math.sqrt(HDIM)
    key_id = lax.broadcasted_iota(jnp.int32, (1, window), 1)

    def cached(j):
        return jnp.concatenate([pool[off_s[j] + b] for b in range(MAXB)], axis=0)

    def attend(items, caches, lens):
        added = [x[rows:] for x in items]
        new_keys = [x.astype(jnp.bfloat16) for x in added]
        new_values = [pltpu.roll(x, steps, 0).astype(jnp.bfloat16) for x in added]
        items = [x[:rows].astype(jnp.bfloat16) for x in items]
        scores, fresh = [], []
        for x, y, cache, size in zip(items, new_keys, caches, lens):
            s = lax.dot_general(
                x, cache()[:, :HDIM], NT, preferred_element_type=jnp.float32
            )
            scores.append(jnp.where(key_id < size * BLK, s, -jnp.inf))
            s = lax.dot_general(x, y, NT, preferred_element_type=jnp.float32)
            fresh.append(s + causal[...])
        tops = [
            jnp.maximum(jnp.max(s, axis=1, keepdims=True), jnp.max(f, axis=1, keepdims=True))
            for s, f in zip(scores, fresh)
        ]
        scores = [jnp.exp2((s - m) * factor) for s, m in zip(scores, tops)]
        fresh = [jnp.exp2((f - m) * factor) for f, m in zip(fresh, tops)]
        results = []
        for y, s, f, cache in zip(new_values, scores, fresh, caches):
            total = jnp.sum(s, axis=1, keepdims=True) + jnp.sum(f, axis=1, keepdims=True)
            o = jnp.dot(
                s.astype(jnp.bfloat16), cache()[:, HDIM:],
                preferred_element_type=jnp.float32,
            )
            o = o + jnp.dot(
                f.astype(jnp.bfloat16), y, preferred_element_type=jnp.float32
            )
            results.append(o / total)
        return results

    def attend_own(items, owners):
        return attend(
            items,
            [functools.partial(cached, j) for j in owners],
            [len_s[me, j] for j in owners],
        )

    def put(i, value):
        res[i] = value

    def stay_group(indices):
        owners = [stay_s[i] for i in indices]
        for i, o in zip(indices, attend_own([item_of(j) for j in owners], owners)):
            put(i, o)

    def move_group(ks):
        owners = [slot_s[k] for k in ks]
        sent = [(used_s[k] > 0) & jnp.logical_not(is_late & (push_k == k)) for k in ks]
        items = [
            jnp.where(ok, q_got[k].astype(jnp.float32), item_of(j))
            for k, j, ok in zip(ks, owners, sent)
        ]
        for k, o in zip(ks, attend_own(items, owners)):
            put(stays + k, o)
            r_out[k] = o.astype(jnp.bfloat16)
        for i in range(len(ks)):
            k = upper * ks[len(ks) - 1 - i] + (1 - upper) * ks[i]

            @pl.when(jnp.logical_not(is_late & (push_k == k)))
            def _():
                send_r(k).start()

    pl.when(meet_at == 0)(meet)
    copy_pool.wait()
    for copy in copy_w:
        copy.start()

    @pl.when(is_late)
    def _():
        push_out[...] = pool[off_s[push_slot] + tp]
        push.start()

    def stay_step(g, carry):
        stay_group([g * group + u for u in range(group)])

        pl.when(meet_at == g + 1)(meet)
        return carry

    lax.fori_loop(0, full, stay_step, 0)
    if stays > full * group:
        stay_group(list(range(full * group, stays)))

    def arrived(count, batch):
        if count > 0:
            got = q_got.at[pl.ds(0, count)]
            pltpu.make_async_copy(got, got, q_recv.at[batch]).wait()

    def serve_near():
        arrived(band - 1, 0)

        def rotation(i):
            other = i + lax.div(i + band - place, band)
            return lax.rem(other - place - 1 + n, n)

        grouped(band - 1, 7, lambda idx: move_group([rotation(i) for i in idx]))

    def far_rotation(i):
        owner = upper * (band - 1 - i) + (1 - upper) * (band + i)
        return lax.rem(owner - me - 1 + n, n)

    def serve_shallow():
        arrived(band - 1, 1)
        grouped(band - 1, 7, lambda idx: move_group([far_rotation(i) for i in idx]))

    def serve_deep():
        pl.when(jnp.logical_not(is_late))(lambda: arrived(1, 2))
        move_group([far_rotation(band - 1)])

    def serve(step):
        if crowded and step == 1:

            @pl.when(upper > 0)
            def _():
                pl.when(jnp.logical_not(is_late))(serve_deep)
                serve_near()
                serve_shallow()

            @pl.when((upper == 0) & jnp.logical_not(is_early))
            def _():
                serve_near()
                serve_shallow()

        elif crowded and step == 2:

            @pl.when(is_early)
            def _():
                serve_near()
                serve_shallow()

            pl.when(upper == 0)(serve_deep)
        elif not crowded and step == 0:
            serve_near()
            serve_shallow()
            serve_deep()

    serve(0)

    def gather(j, carry):
        own_rows = res[pos_s[j]]
        fin[pl.ds(pl.multiple_of(j * rows, 8), rows), :] = jnp.where(
            shift_s[j] > 0, jnp.zeros_like(own_rows), own_rows
        )
        return carry

    lax.fori_loop(0, slots, gather, 0, unroll=8)
    for t in range(steps):
        for h in range(heads):
            lhs[t * slots : (t + 1) * slots, h * HDIM : (h + 1) * HDIM] = fin[
                pl.ds(t * heads + h, slots, stride=rows), :
            ].astype(jnp.bfloat16)
    for c in range(chunks):
        copy_w[c].wait()
    for c in range(chunks):
        o_out[c] = jnp.dot(lhs[...], w_buf[c], preferred_element_type=jnp.float32).astype(
            jnp.bfloat16
        )
    send_o.start()

    serve(1)
    for c in range(chunks):
        copy_w[chunks + c].wait()
    for c in range(chunks):
        main[c] = jnp.dot(lhs[...], w_buf[chunks + c], preferred_element_type=jnp.float32)

    pad = back.shape[0]
    row_id = lax.broadcasted_iota(jnp.int32, (slots, steps * pad), 0)
    col_id = lax.broadcasted_iota(jnp.int32, (slots, steps * pad), 1)
    turns = jnp.zeros((slots, steps * pad), jnp.int32)
    for j in range(slots):
        turns = jnp.where(row_id == j, shift_s[j], turns)
    for t in range(steps):
        spread[t * slots : (t + 1) * slots, :] = jnp.where(
            (turns > 0) & (col_id == turns + (t * pad - 1)), 1.0, 0.0
        ).astype(jnp.bfloat16)

    serve(2)

    @pl.when(is_early)
    def _():
        push.wait_recv()
        relay.start()

    @pl.when(is_early)
    def _():
        relay.wait_recv()
        (o,) = attend(
            [item_of(push_slot)],
            [lambda: jnp.concatenate([push_got[b] for b in range(MAXB)], axis=0)],
            [len_s[mirror, push_slot]],
        )
        r_got[push_k] = o.astype(jnp.bfloat16)

    all_but_one(is_early, r_got, r_recv)
    for k in range(peers, pad):
        back[k] = jnp.zeros((rows, HDIM), jnp.float32)
    for k in range(peers):
        back[k] = r_got[k].astype(jnp.float32)
    flat_back = back.reshape(pad * rows, HDIM)
    for t in range(steps):
        for h in range(heads):
            moved_lhs[t * pad : (t + 1) * pad, h * HDIM : (h + 1) * HDIM] = flat_back[
                pl.ds(t * heads + h, pad, stride=rows), :
            ]
    moved = moved_lhs[...].astype(jnp.bfloat16)
    for c in range(chunks):
        m_out[c] = jnp.dot(moved, w_buf[c], preferred_element_type=jnp.float32).astype(
            jnp.bfloat16
        )
    send_m.start()
    send_o.wait_recv()
    for c in range(chunks):
        own[c] = jnp.dot(moved, w_buf[chunks + c], preferred_element_type=jnp.float32)
        main[c] = main[c] + o_got[c].astype(jnp.float32)
    send_m.wait_recv()
    for c in range(chunks):
        total = (own[c] + m_got[c].astype(jnp.float32)).astype(jnp.bfloat16)
        total = jnp.dot(spread[...], total, preferred_element_type=jnp.float32)
        total = (total + main[c]).astype(out_ref.dtype)
        for t in range(steps):
            out_ref[t, :, c * cols : (c + 1) * cols] = total[t * slots : (t + 1) * slots]
    all_but_one(is_early, q_out, q_send)
    all_but_one(is_late, r_out, r_send)
    send_o.wait_send()
    send_m.wait_send()

    @pl.when(is_late)
    def _():
        push.wait_send()

    @pl.when(is_early)
    def _():
        relay.wait_send()


def body(n, queries, new_kv, cache_pool, lengths, anchor, out_weight):
    steps, slots, width = queries.shape
    features = out_weight.shape[1]
    half = features // lax.axis_size("tp")
    cols = 768 if half % 768 == 0 else half
    chunks = half // cols
    rows = steps * (width // HDIM)
    span = rows + 2 * steps
    peers = n - 1
    pad = -(-peers // 8) * 8
    blocks = cache_pool.shape[0] // BLK
    edge = min(1, n // 4)
    bf16, f32, i32 = jnp.bfloat16, jnp.float32, jnp.int32
    dma = pltpu.SemaphoreType.DMA
    anywhere = pl.BlockSpec(memory_space=pltpu.HBM)
    cache = cache_pool.reshape(blocks, BLK, 2 * HDIM)
    queries, new_kv, cache, lengths, anchor, out_weight = (
        pltpu.with_memory_space_constraint(x, pltpu.HBM)
        for x in (queries, new_kv, cache, lengths, anchor, out_weight)
    )
    return pl.pallas_call(
        functools.partial(kernel, n, edge, cols),
        out_shape=jax.ShapeDtypeStruct((steps, slots, half), bf16),
        in_specs=[anywhere] * 6,
        out_specs=pl.BlockSpec(memory_space=pltpu.VMEM),
        scratch_shapes=[
            pltpu.VMEM(queries.shape, bf16),
            pltpu.VMEM(new_kv.shape, bf16),
            pltpu.VMEM((blocks + MAXB - 1, BLK, 2 * HDIM), bf16),
            pltpu.VMEM((2 * chunks, width, cols), bf16),
            pltpu.VMEM((slots, span, HDIM), f32),
            pltpu.VMEM((slots, rows, HDIM), f32),
            pltpu.VMEM((slots * rows, HDIM), f32),
            pltpu.VMEM((steps * slots, width), bf16),
            pltpu.VMEM((rows, 2 * steps), f32),
            pltpu.VMEM((peers, span, HDIM), bf16),
            pltpu.VMEM((peers, span, HDIM), bf16),
            pltpu.VMEM((peers, rows, HDIM), bf16),
            pltpu.VMEM((peers, rows, HDIM), bf16),
            pltpu.VMEM((chunks, steps * slots, cols), bf16),
            pltpu.VMEM((chunks, steps * slots, cols), bf16),
            pltpu.VMEM((chunks, steps * pad, cols), bf16),
            pltpu.VMEM((chunks, steps * pad, cols), bf16),
            pltpu.VMEM((chunks, steps * slots, cols), f32),
            pltpu.VMEM((chunks, steps * pad, cols), f32),
            pltpu.VMEM((pad, rows, HDIM), f32),
            pltpu.VMEM((steps * pad, width), f32),
            pltpu.VMEM((steps * slots, steps * pad), bf16),
            pltpu.VMEM((BLK, 2 * HDIM), bf16),
            pltpu.VMEM((MAXB, BLK, 2 * HDIM), bf16),
        ]
        + [pltpu.SMEM(lengths.shape, i32), pltpu.SMEM(anchor.shape, i32)]
        + [pltpu.SMEM((max(slots, n),), i32)] * 8
        + [dma((5,)), dma((2 * chunks,))]
        + [dma(()), dma((3,)), dma(()), dma(())]
        + [dma((2,)), dma(()), dma(()), dma((3,))],
        compiler_params=pltpu.CompilerParams(
            collective_id=0, has_side_effects=True, vmem_limit_bytes=48 * 1024 * 1024
        ),
    )(queries, new_kv, cache, lengths, anchor, out_weight)


def solution(mesh):
    n = mesh.shape["inst"]
    placed = (
        P(None, ("groups", "inst"), "tp"),
        P(None, ("groups", "inst"), None),
        P(("groups", "inst"), None),
        P("groups", None),
        P("groups", None),
        P("tp", None),
    )
    return jax.shard_map(
        functools.partial(body, n),
        mesh=mesh,
        in_specs=placed,
        out_specs=P(None, ("groups", "inst"), "tp"),
        check_vma=False,
    )
```

```python
import functools
import math

import jax
import jax.numpy as jnp
from jax import lax
from jax.experimental import pallas as pl
from jax.experimental.pallas import tpu as pltpu
from jax.sharding import PartitionSpec as P

HDIM = 128
BLK = 128
MAXB = 2
MESH = pl.DeviceIdType.MESH
NT = (((1,), (1,)), ((), ()))


def grouped(count, unroll, fn):
    full = count // unroll
    if full == 1:
        fn([i for i in range(unroll)])
    elif full > 1:

        def step(g, carry):
            fn([g * unroll + u for u in range(unroll)])
            return carry

        lax.fori_loop(0, full, step, 0)
    rest = list(range(full * unroll, count))
    if rest:
        fn(rest)


def kernel(
    n, edge, cols, q_hbm, kv_hbm, pool_hbm, len_hbm, anc_hbm, w_hbm, out_ref,
    q_in, kv_in, pool, w_buf, item, res, fin, lhs, causal,
    q_out, q_got, r_out, r_got, o_out, o_got, m_out, m_got, main, own, back, moved_lhs, spread,
    push_out, push_got,
    len_s, anc_s, shift_s, off_s, stay_s, nxt_s, slot_s, used_s, free_s, pos_s,
    in_sem, w_sem, q_send, q_recv, r_send, r_recv, x_send, o_recv, m_recv, p_sem,
):
    steps, slots, width = q_in.shape
    heads = width // HDIM
    rows = steps * heads
    span = rows + 2 * steps
    window = MAXB * BLK
    blocks = pool_hbm.shape[0]
    half = out_ref.shape[2]
    chunks = half // cols
    peers = n - 1
    stays = slots - peers
    me = lax.axis_index("inst")
    tp = lax.axis_index("tp")
    crowded = peers <= slots // 4
    mirror = n - 1 - me
    is_early = me < edge
    is_late = mirror < edge
    push_k = 0
    band = n // 2
    upper = lax.div(me, band)
    place = lax.rem(me, band)
    deepest = lax.div(lax.rem(me + n - 1, n) + 2, n)

    copy_len = pltpu.make_async_copy(len_hbm, len_s, in_sem.at[0])
    copy_anc = pltpu.make_async_copy(anc_hbm, anc_s, in_sem.at[1])
    copy_q = pltpu.make_async_copy(q_hbm, q_in, in_sem.at[2])
    copy_kv = pltpu.make_async_copy(kv_hbm, kv_in, in_sem.at[3])
    copy_pool = pltpu.make_async_copy(pool_hbm, pool.at[pl.ds(0, blocks)], in_sem.at[4])
    copy_len.start()
    copy_anc.start()
    copy_q.start()
    copy_kv.start()
    copy_pool.start()
    copy_w = []
    for c in range(2 * chunks):
        side = (1 - tp) if c < chunks else tp
        column = pl.multiple_of(side * half + (c % chunks) * cols, cols)
        copy_w.append(
            pltpu.make_async_copy(w_hbm.at[:, pl.ds(column, cols)], w_buf.at[c], w_sem.at[c])
        )

    def peer(k):
        return {"inst": lax.rem(me + k, n)}

    barrier = pltpu.get_barrier_semaphore()
    for k in range(peers):

        @pl.when(jnp.logical_not(is_late & (push_k == k)))
        def _():
            pl.semaphore_signal(barrier, inc=1, device_id=peer(k + 1), device_id_type=MESH)

    pl.semaphore_signal(barrier, inc=1, device_id={"tp": 1 - tp}, device_id_type=MESH)

    def scan_slot(j, carry):
        off, found = carry
        turn = me - anc_s[me, j]
        turn = jnp.where(turn < 0, turn + n, turn)
        shift_s[j] = turn
        off_s[j] = off
        found = tuple(jnp.where(turn == k + 1, j, found[k]) for k in range(peers))
        return off + len_s[me, j], found

    copy_len.wait()
    copy_anc.wait()
    _, found = lax.fori_loop(
        0, slots, scan_slot, (jnp.int32(0), tuple(jnp.int32(-1) for _ in range(peers))),
        unroll=8,
    )

    flat = item.reshape(slots * span, HDIM)
    copy_q.wait()
    copy_kv.wait()
    for t in range(steps):
        for h in range(heads):
            flat[pl.ds(t * heads + h, slots, stride=span), :] = q_in[
                t, :, h * HDIM : (h + 1) * HDIM
            ].astype(jnp.float32)
        for part in range(2):
            flat[pl.ds(rows + part * steps + t, slots, stride=span), :] = kv_in[
                t, :, part * HDIM : (part + 1) * HDIM
            ].astype(jnp.float32)

    def item_of(slot):
        return item[slot]

    for k in range(peers):
        q_out[k] = item_of(jnp.maximum(found[k], 0)).astype(jnp.bfloat16)

    def batch_to(k):
        across = lax.rem(lax.div(lax.rem(me + n - 1 - k, n), band) + upper, 2)
        return across * (1 + deepest)

    def send_q(k):
        return pltpu.make_async_remote_copy(
            src_ref=q_out.at[k], dst_ref=q_got.at[k], send_sem=q_send,
            recv_sem=q_recv.at[batch_to(k)], device_id=peer(n - 1 - k), device_id_type=MESH,
        )

    def send_r(k):
        return pltpu.make_async_remote_copy(
            src_ref=r_out.at[k], dst_ref=r_got.at[k], send_sem=r_send,
            recv_sem=r_recv, device_id=peer(k + 1), device_id_type=MESH,
        )

    send_o = pltpu.make_async_remote_copy(
        src_ref=o_out, dst_ref=o_got, send_sem=x_send.at[0],
        recv_sem=o_recv, device_id={"tp": 1 - tp}, device_id_type=MESH,
    )
    send_m = pltpu.make_async_remote_copy(
        src_ref=m_out, dst_ref=m_got, send_sem=x_send.at[1],
        recv_sem=m_recv, device_id={"tp": 1 - tp}, device_id_type=MESH,
    )
    push = pltpu.make_async_remote_copy(
        src_ref=push_out, dst_ref=push_got.at[tp], send_sem=p_sem.at[0],
        recv_sem=p_sem.at[1], device_id={"inst": mirror}, device_id_type=MESH,
    )
    relay = pltpu.make_async_remote_copy(
        src_ref=push_got.at[tp], dst_ref=push_got.at[tp], send_sem=p_sem.at[0],
        recv_sem=p_sem.at[2], device_id={"tp": 1 - tp}, device_id_type=MESH,
    )

    group = 5
    full = stays // group

    def all_but_one(fewer, ref, sem):
        @pl.when(fewer)
        def _():
            if peers > 1:
                part = ref.at[pl.ds(0, peers - 1)]
                pltpu.make_async_copy(part, part, sem).wait()

        @pl.when(jnp.logical_not(fewer))
        def _():
            pltpu.make_async_copy(ref, ref, sem).wait()

    def greet():
        pl.semaphore_wait(barrier, jnp.where(is_early, n - 1, n))

    def send_all_q():
        for k in range(peers):

            @pl.when(jnp.logical_not(is_early & (push_k == k)))
            def _():
                send_q(k).start()

    def meet():
        greet()
        send_all_q()

    meet_at = jnp.where(me == 0, full, jnp.clip((mirror - 1) // 2 * 2 - 1, 0, full))

    for k in range(peers):
        slot_s[k] = jnp.maximum(found[k], 0)
    push_slot = slot_s[push_k]

    def scan_next(i, cur):
        j = slots - 1 - i
        cur = jnp.where(shift_s[j] == 0, j, cur)
        nxt_s[j] = cur
        return cur

    lax.fori_loop(0, slots, scan_next, jnp.int32(slots - 1), unroll=True)

    def scan_stay(i, cur):
        stay_s[i] = cur
        return nxt_s[jnp.minimum(cur + 1, slots - 1)]

    lax.fori_loop(0, slots, scan_stay, nxt_s[0], unroll=True)
    spare = jnp.int32(0)
    for k in range(peers):
        slot_s[k] = jnp.where(found[k] >= 0, found[k], stay_s[stays + spare])
        used_s[k] = jnp.where(found[k] >= 0, 1, 0)
        spare = spare + jnp.where(found[k] >= 0, 0, 1)
    nxt = jnp.int32(peers - 1)
    for k in reversed(range(peers)):
        nxt = jnp.where(found[k] >= 0, nxt, k)
        nxt_s[k] = nxt
    nxt = nxt_s[0]
    for k in range(peers):
        free_s[k] = nxt
        nxt = nxt_s[jnp.minimum(nxt + 1, peers - 1)]

    def scan_pos(j, count):
        turn = shift_s[j]
        extra = free_s[jnp.clip(count - stays, 0, peers - 1)]
        rest = jnp.where(count < stays, count, stays + extra)
        pos_s[j] = jnp.where(turn > 0, stays + turn - 1, rest)
        return count + jnp.where(turn > 0, 0, 1)

    lax.fori_loop(0, slots, scan_pos, jnp.int32(0), unroll=True)

    pool[blocks] = jnp.zeros((BLK, 2 * HDIM), pool.dtype)
    row_id = lax.broadcasted_iota(jnp.int32, (rows, 2 * steps), 0)
    col_id = lax.broadcasted_iota(jnp.int32, (rows, 2 * steps), 1)
    causal[...] = jnp.where((col_id < steps) & (row_id >= col_id * heads), 0.0, -jnp.inf)

    factor = math.log2(math.e) / math.sqrt(HDIM)
    key_id = lax.broadcasted_iota(jnp.int32, (1, window), 1)

    def cached(j):
        return jnp.concatenate([pool[off_s[j] + b] for b in range(MAXB)], axis=0)

    def attend(items, caches, lens):
        added = [x[rows:] for x in items]
        new_keys = [x.astype(jnp.bfloat16) for x in added]
        new_values = [pltpu.roll(x, steps, 0).astype(jnp.bfloat16) for x in added]
        items = [x[:rows].astype(jnp.bfloat16) for x in items]
        scores, fresh = [], []
        for x, y, cache, size in zip(items, new_keys, caches, lens):
            s = lax.dot_general(
                x, cache()[:, :HDIM], NT, preferred_element_type=jnp.float32
            )
            scores.append(jnp.where(key_id < size * BLK, s, -jnp.inf))
            s = lax.dot_general(x, y, NT, preferred_element_type=jnp.float32)
            fresh.append(s + causal[...])
        tops = [
            jnp.maximum(jnp.max(s, axis=1, keepdims=True), jnp.max(f, axis=1, keepdims=True))
            for s, f in zip(scores, fresh)
        ]
        scores = [jnp.exp2((s - m) * factor) for s, m in zip(scores, tops)]
        fresh = [jnp.exp2((f - m) * factor) for f, m in zip(fresh, tops)]
        results = []
        for y, s, f, cache in zip(new_values, scores, fresh, caches):
            total = jnp.sum(s, axis=1, keepdims=True) + jnp.sum(f, axis=1, keepdims=True)
            o = jnp.dot(
                s.astype(jnp.bfloat16), cache()[:, HDIM:],
                preferred_element_type=jnp.float32,
            )
            o = o + jnp.dot(
                f.astype(jnp.bfloat16), y, preferred_element_type=jnp.float32
            )
            results.append(o / total)
        return results

    def attend_own(items, owners):
        return attend(
            items,
            [functools.partial(cached, j) for j in owners],
            [len_s[me, j] for j in owners],
        )

    def put(i, value):
        res[i] = value

    def stay_group(indices):
        owners = [stay_s[i] for i in indices]
        for i, o in zip(indices, attend_own([item_of(j) for j in owners], owners)):
            put(i, o)

    def move_group(ks):
        owners = [slot_s[k] for k in ks]
        sent = [(used_s[k] > 0) & jnp.logical_not(is_late & (push_k == k)) for k in ks]
        items = [
            jnp.where(ok, q_got[k].astype(jnp.float32), item_of(j))
            for k, j, ok in zip(ks, owners, sent)
        ]
        for k, o in zip(ks, attend_own(items, owners)):
            put(stays + k, o)
            r_out[k] = o.astype(jnp.bfloat16)
        for i in range(len(ks)):
            k = upper * ks[len(ks) - 1 - i] + (1 - upper) * ks[i]

            @pl.when(jnp.logical_not(is_late & (push_k == k)))
            def _():
                send_r(k).start()

    pl.when(meet_at == 0)(meet)
    copy_pool.wait()
    for copy in copy_w:
        copy.start()

    @pl.when(is_late)
    def _():
        push_out[...] = pool[off_s[push_slot] + tp]
        push.start()

    def stay_step(g, carry):
        stay_group([g * group + u for u in range(group)])

        pl.when(meet_at == g + 1)(meet)
        return carry

    lax.fori_loop(0, full, stay_step, 0)
    if stays > full * group:
        stay_group(list(range(full * group, stays)))

    def arrived(count, batch):
        if count > 0:
            got = q_got.at[pl.ds(0, count)]
            pltpu.make_async_copy(got, got, q_recv.at[batch]).wait()

    def serve_near():
        arrived(band - 1, 0)

        def rotation(i):
            other = i + lax.div(i + band - place, band)
            return lax.rem(other - place - 1 + n, n)

        grouped(band - 1, 7, lambda idx: move_group([rotation(i) for i in idx]))

    def far_rotation(i):
        owner = upper * (band - 1 - i) + (1 - upper) * (band + i)
        return lax.rem(owner - me - 1 + n, n)

    def serve_shallow():
        arrived(band - 1, 1)
        grouped(band - 1, 7, lambda idx: move_group([far_rotation(i) for i in idx]))

    def serve_deep():
        pl.when(jnp.logical_not(is_late))(lambda: arrived(1, 2))
        move_group([far_rotation(band - 1)])

    def serve(step):
        if crowded and step == 1:

            @pl.when(upper > 0)
            def _():
                pl.when(jnp.logical_not(is_late))(serve_deep)
                serve_shallow()
                serve_near()

            @pl.when((upper == 0) & jnp.logical_not(is_early))
            def _():
                serve_near()
                serve_shallow()

        elif crowded and step == 2:

            @pl.when(is_early)
            def _():
                serve_near()
                serve_shallow()

            pl.when(upper == 0)(serve_deep)
        elif not crowded and step == 0:
            serve_near()
            serve_shallow()
            serve_deep()

    serve(0)

    def gather(j, carry):
        own_rows = res[pos_s[j]]
        fin[pl.ds(pl.multiple_of(j * rows, 8), rows), :] = jnp.where(
            shift_s[j] > 0, jnp.zeros_like(own_rows), own_rows
        )
        return carry

    lax.fori_loop(0, slots, gather, 0, unroll=8)
    for t in range(steps):
        for h in range(heads):
            lhs[t * slots : (t + 1) * slots, h * HDIM : (h + 1) * HDIM] = fin[
                pl.ds(t * heads + h, slots, stride=rows), :
            ].astype(jnp.bfloat16)
    for c in range(chunks):
        copy_w[c].wait()
    for c in range(chunks):
        o_out[c] = jnp.dot(lhs[...], w_buf[c], preferred_element_type=jnp.float32).astype(
            jnp.bfloat16
        )
    send_o.start()

    serve(1)
    for c in range(chunks):
        copy_w[chunks + c].wait()
    for c in range(chunks):
        main[c] = jnp.dot(lhs[...], w_buf[chunks + c], preferred_element_type=jnp.float32)

    pad = back.shape[0]
    row_id = lax.broadcasted_iota(jnp.int32, (slots, steps * pad), 0)
    col_id = lax.broadcasted_iota(jnp.int32, (slots, steps * pad), 1)
    turns = jnp.zeros((slots, steps * pad), jnp.int32)
    for j in range(slots):
        turns = jnp.where(row_id == j, shift_s[j], turns)
    for t in range(steps):
        spread[t * slots : (t + 1) * slots, :] = jnp.where(
            (turns > 0) & (col_id == turns + (t * pad - 1)), 1.0, 0.0
        ).astype(jnp.bfloat16)

    serve(2)

    @pl.when(is_early)
    def _():
        push.wait_recv()
        relay.start()

    @pl.when(is_early)
    def _():
        relay.wait_recv()
        (o,) = attend(
            [item_of(push_slot)],
            [lambda: jnp.concatenate([push_got[b] for b in range(MAXB)], axis=0)],
            [len_s[mirror, push_slot]],
        )
        r_got[push_k] = o.astype(jnp.bfloat16)

    all_but_one(is_early, r_got, r_recv)
    for k in range(peers, pad):
        back[k] = jnp.zeros((rows, HDIM), jnp.float32)
    for k in range(peers):
        back[k] = r_got[k].astype(jnp.float32)
    flat_back = back.reshape(pad * rows, HDIM)
    for t in range(steps):
        for h in range(heads):
            moved_lhs[t * pad : (t + 1) * pad, h * HDIM : (h + 1) * HDIM] = flat_back[
                pl.ds(t * heads + h, pad, stride=rows), :
            ]
    moved = moved_lhs[...].astype(jnp.bfloat16)
    for c in range(chunks):
        m_out[c] = jnp.dot(moved, w_buf[c], preferred_element_type=jnp.float32).astype(
            jnp.bfloat16
        )
    send_m.start()
    send_o.wait_recv()
    for c in range(chunks):
        own[c] = jnp.dot(moved, w_buf[chunks + c], preferred_element_type=jnp.float32)
        main[c] = main[c] + o_got[c].astype(jnp.float32)
    send_m.wait_recv()
    for c in range(chunks):
        total = (own[c] + m_got[c].astype(jnp.float32)).astype(jnp.bfloat16)
        total = jnp.dot(spread[...], total, preferred_element_type=jnp.float32)
        total = (total + main[c]).astype(out_ref.dtype)
        for t in range(steps):
            out_ref[t, :, c * cols : (c + 1) * cols] = total[t * slots : (t + 1) * slots]
    all_but_one(is_early, q_out, q_send)
    all_but_one(is_late, r_out, r_send)
    send_o.wait_send()
    send_m.wait_send()

    @pl.when(is_late)
    def _():
        push.wait_send()

    @pl.when(is_early)
    def _():
        relay.wait_send()


def body(n, queries, new_kv, cache_pool, lengths, anchor, out_weight):
    steps, slots, width = queries.shape
    features = out_weight.shape[1]
    half = features // lax.axis_size("tp")
    cols = 768 if half % 768 == 0 else half
    chunks = half // cols
    rows = steps * (width // HDIM)
    span = rows + 2 * steps
    peers = n - 1
    pad = -(-peers // 8) * 8
    blocks = cache_pool.shape[0] // BLK
    edge = min(1, n // 4)
    bf16, f32, i32 = jnp.bfloat16, jnp.float32, jnp.int32
    dma = pltpu.SemaphoreType.DMA
    anywhere = pl.BlockSpec(memory_space=pltpu.HBM)
    cache = cache_pool.reshape(blocks, BLK, 2 * HDIM)
    queries, new_kv, cache, lengths, anchor, out_weight = (
        pltpu.with_memory_space_constraint(x, pltpu.HBM)
        for x in (queries, new_kv, cache, lengths, anchor, out_weight)
    )
    return pl.pallas_call(
        functools.partial(kernel, n, edge, cols),
        out_shape=jax.ShapeDtypeStruct((steps, slots, half), bf16),
        in_specs=[anywhere] * 6,
        out_specs=pl.BlockSpec(memory_space=pltpu.VMEM),
        scratch_shapes=[
            pltpu.VMEM(queries.shape, bf16),
            pltpu.VMEM(new_kv.shape, bf16),
            pltpu.VMEM((blocks + MAXB - 1, BLK, 2 * HDIM), bf16),
            pltpu.VMEM((2 * chunks, width, cols), bf16),
            pltpu.VMEM((slots, span, HDIM), f32),
            pltpu.VMEM((slots, rows, HDIM), f32),
            pltpu.VMEM((slots * rows, HDIM), f32),
            pltpu.VMEM((steps * slots, width), bf16),
            pltpu.VMEM((rows, 2 * steps), f32),
            pltpu.VMEM((peers, span, HDIM), bf16),
            pltpu.VMEM((peers, span, HDIM), bf16),
            pltpu.VMEM((peers, rows, HDIM), bf16),
            pltpu.VMEM((peers, rows, HDIM), bf16),
            pltpu.VMEM((chunks, steps * slots, cols), bf16),
            pltpu.VMEM((chunks, steps * slots, cols), bf16),
            pltpu.VMEM((chunks, steps * pad, cols), bf16),
            pltpu.VMEM((chunks, steps * pad, cols), bf16),
            pltpu.VMEM((chunks, steps * slots, cols), f32),
            pltpu.VMEM((chunks, steps * pad, cols), f32),
            pltpu.VMEM((pad, rows, HDIM), f32),
            pltpu.VMEM((steps * pad, width), f32),
            pltpu.VMEM((steps * slots, steps * pad), bf16),
            pltpu.VMEM((BLK, 2 * HDIM), bf16),
            pltpu.VMEM((MAXB, BLK, 2 * HDIM), bf16),
        ]
        + [pltpu.SMEM(lengths.shape, i32), pltpu.SMEM(anchor.shape, i32)]
        + [pltpu.SMEM((max(slots, n),), i32)] * 8
        + [dma((5,)), dma((2 * chunks,))]
        + [dma(()), dma((3,)), dma(()), dma(())]
        + [dma((2,)), dma(()), dma(()), dma((3,))],
        compiler_params=pltpu.CompilerParams(
            collective_id=0, has_side_effects=True, vmem_limit_bytes=48 * 1024 * 1024
        ),
    )(queries, new_kv, cache, lengths, anchor, out_weight)


def solution(mesh):
    n = mesh.shape["inst"]
    placed = (
        P(None, ("groups", "inst"), "tp"),
        P(None, ("groups", "inst"), None),
        P(("groups", "inst"), None),
        P("groups", None),
        P("groups", None),
        P("tp", None),
    )
    return jax.shard_map(
        functools.partial(body, n),
        mesh=mesh,
        in_specs=placed,
        out_specs=P(None, ("groups", "inst"), "tp"),
        check_vma=False,
    )
```

```python
import functools
import math

import jax
import jax.numpy as jnp
from jax import lax
from jax.experimental import pallas as pl
from jax.experimental.pallas import tpu as pltpu
from jax.sharding import PartitionSpec as P

HDIM = 128
BLK = 128
MAXB = 2
MESH = pl.DeviceIdType.MESH
NT = (((1,), (1,)), ((), ()))


def grouped(count, unroll, fn):
    full = count // unroll
    if full == 1:
        fn([i for i in range(unroll)])
    elif full > 1:

        def step(g, carry):
            fn([g * unroll + u for u in range(unroll)])
            return carry

        lax.fori_loop(0, full, step, 0)
    rest = list(range(full * unroll, count))
    if rest:
        fn(rest)


def kernel(
    n, edge, cols, q_hbm, kv_hbm, pool_hbm, len_hbm, anc_hbm, w_hbm, out_ref,
    q_in, kv_in, pool, w_buf, item, res, fin, lhs, causal,
    q_out, q_got, r_out, r_got, o_out, o_got, m_out, m_got, main, own, back, moved_lhs, spread,
    push_out, push_got,
    len_s, anc_s, shift_s, off_s, stay_s, nxt_s, slot_s, used_s, free_s, pos_s,
    in_sem, w_sem, q_send, q_recv, r_send, r_recv, x_send, o_recv, m_recv, p_sem,
):
    steps, slots, width = q_in.shape
    heads = width // HDIM
    rows = steps * heads
    span = rows + 2 * steps
    window = MAXB * BLK
    blocks = pool_hbm.shape[0]
    half = out_ref.shape[2]
    chunks = half // cols
    peers = n - 1
    stays = slots - peers
    me = lax.axis_index("inst")
    tp = lax.axis_index("tp")
    crowded = peers <= slots // 4
    mirror = n - 1 - me
    is_early = me < edge
    is_late = mirror < edge
    push_k = 0
    band = n // 2
    upper = lax.div(me, band)
    place = lax.rem(me, band)
    deepest = lax.div(lax.rem(me + n - 1, n) + 2, n)

    def peer(k):
        return {"inst": lax.rem(me + k, n)}

    barrier = pltpu.get_barrier_semaphore()
    for k in range(peers):

        @pl.when(jnp.logical_not(is_late & (push_k == k)))
        def _():
            pl.semaphore_signal(barrier, inc=1, device_id=peer(k + 1), device_id_type=MESH)

    pl.semaphore_signal(barrier, inc=1, device_id={"tp": 1 - tp}, device_id_type=MESH)

    copy_len = pltpu.make_async_copy(len_hbm, len_s, in_sem.at[0])
    copy_anc = pltpu.make_async_copy(anc_hbm, anc_s, in_sem.at[1])
    copy_q = pltpu.make_async_copy(q_hbm, q_in, in_sem.at[2])
    copy_kv = pltpu.make_async_copy(kv_hbm, kv_in, in_sem.at[3])
    copy_pool = pltpu.make_async_copy(pool_hbm, pool.at[pl.ds(0, blocks)], in_sem.at[4])
    copy_len.start()
    copy_anc.start()
    copy_q.start()
    copy_kv.start()
    copy_pool.start()
    copy_w = []
    for c in range(2 * chunks):
        side = (1 - tp) if c < chunks else tp
        column = pl.multiple_of(side * half + (c % chunks) * cols, cols)
        copy_w.append(
            pltpu.make_async_copy(w_hbm.at[:, pl.ds(column, cols)], w_buf.at[c], w_sem.at[c])
        )

    def scan_slot(j, carry):
        off, found = carry
        turn = me - anc_s[me, j]
        turn = jnp.where(turn < 0, turn + n, turn)
        shift_s[j] = turn
        off_s[j] = off
        found = tuple(jnp.where(turn == k + 1, j, found[k]) for k in range(peers))
        return off + len_s[me, j], found

    copy_len.wait()
    copy_anc.wait()
    _, found = lax.fori_loop(
        0, slots, scan_slot, (jnp.int32(0), tuple(jnp.int32(-1) for _ in range(peers))),
        unroll=8,
    )

    flat = item.reshape(slots * span, HDIM)
    copy_q.wait()
    copy_kv.wait()
    for t in range(steps):
        for h in range(heads):
            flat[pl.ds(t * heads + h, slots, stride=span), :] = q_in[
                t, :, h * HDIM : (h + 1) * HDIM
            ].astype(jnp.float32)
        for part in range(2):
            flat[pl.ds(rows + part * steps + t, slots, stride=span), :] = kv_in[
                t, :, part * HDIM : (part + 1) * HDIM
            ].astype(jnp.float32)

    def item_of(slot):
        return item[slot]

    for k in range(peers):
        q_out[k] = item_of(jnp.maximum(found[k], 0)).astype(jnp.bfloat16)

    def batch_to(k):
        across = lax.rem(lax.div(lax.rem(me + n - 1 - k, n), band) + upper, 2)
        return across * (1 + deepest)

    def send_q(k):
        return pltpu.make_async_remote_copy(
            src_ref=q_out.at[k], dst_ref=q_got.at[k], send_sem=q_send,
            recv_sem=q_recv.at[batch_to(k)], device_id=peer(n - 1 - k), device_id_type=MESH,
        )

    def send_r(k):
        return pltpu.make_async_remote_copy(
            src_ref=r_out.at[k], dst_ref=r_got.at[k], send_sem=r_send,
            recv_sem=r_recv, device_id=peer(k + 1), device_id_type=MESH,
        )

    send_o = pltpu.make_async_remote_copy(
        src_ref=o_out, dst_ref=o_got, send_sem=x_send.at[0],
        recv_sem=o_recv, device_id={"tp": 1 - tp}, device_id_type=MESH,
    )
    send_m = pltpu.make_async_remote_copy(
        src_ref=m_out, dst_ref=m_got, send_sem=x_send.at[1],
        recv_sem=m_recv, device_id={"tp": 1 - tp}, device_id_type=MESH,
    )
    push = pltpu.make_async_remote_copy(
        src_ref=push_out, dst_ref=push_got.at[tp], send_sem=p_sem.at[0],
        recv_sem=p_sem.at[1], device_id={"inst": mirror}, device_id_type=MESH,
    )
    relay = pltpu.make_async_remote_copy(
        src_ref=push_got.at[tp], dst_ref=push_got.at[tp], send_sem=p_sem.at[0],
        recv_sem=p_sem.at[2], device_id={"tp": 1 - tp}, device_id_type=MESH,
    )

    group = 5
    full = stays // group

    def all_but_one(fewer, ref, sem):
        @pl.when(fewer)
        def _():
            if peers > 1:
                part = ref.at[pl.ds(0, peers - 1)]
                pltpu.make_async_copy(part, part, sem).wait()

        @pl.when(jnp.logical_not(fewer))
        def _():
            pltpu.make_async_copy(ref, ref, sem).wait()

    def greet():
        pl.semaphore_wait(barrier, jnp.where(is_early, n - 1, n))

    def send_all_q():
        for k in range(peers):

            @pl.when(jnp.logical_not(is_early & (push_k == k)))
            def _():
                send_q(k).start()

    def meet():
        greet()
        send_all_q()

    meet_at = jnp.where(me == 0, full, jnp.clip((mirror - 1) // 2 * 2 - 2, 0, full))

    for k in range(peers):
        slot_s[k] = jnp.maximum(found[k], 0)
    push_slot = slot_s[push_k]

    def scan_next(i, cur):
        j = slots - 1 - i
        cur = jnp.where(shift_s[j] == 0, j, cur)
        nxt_s[j] = cur
        return cur

    lax.fori_loop(0, slots, scan_next, jnp.int32(slots - 1), unroll=True)

    def scan_stay(i, cur):
        stay_s[i] = cur
        return nxt_s[jnp.minimum(cur + 1, slots - 1)]

    lax.fori_loop(0, slots, scan_stay, nxt_s[0], unroll=True)
    spare = jnp.int32(0)
    for k in range(peers):
        slot_s[k] = jnp.where(found[k] >= 0, found[k], stay_s[stays + spare])
        used_s[k] = jnp.where(found[k] >= 0, 1, 0)
        spare = spare + jnp.where(found[k] >= 0, 0, 1)
    nxt = jnp.int32(peers - 1)
    for k in reversed(range(peers)):
        nxt = jnp.where(found[k] >= 0, nxt, k)
        nxt_s[k] = nxt
    nxt = nxt_s[0]
    for k in range(peers):
        free_s[k] = nxt
        nxt = nxt_s[jnp.minimum(nxt + 1, peers - 1)]

    def scan_pos(j, count):
        turn = shift_s[j]
        extra = free_s[jnp.clip(count - stays, 0, peers - 1)]
        rest = jnp.where(count < stays, count, stays + extra)
        pos_s[j] = jnp.where(turn > 0, stays + turn - 1, rest)
        return count + jnp.where(turn > 0, 0, 1)

    lax.fori_loop(0, slots, scan_pos, jnp.int32(0), unroll=True)

    pool[blocks] = jnp.zeros((BLK, 2 * HDIM), pool.dtype)
    row_id = lax.broadcasted_iota(jnp.int32, (rows, 2 * steps), 0)
    col_id = lax.broadcasted_iota(jnp.int32, (rows, 2 * steps), 1)
    causal[...] = jnp.where((col_id < steps) & (row_id >= col_id * heads), 0.0, -jnp.inf)

    factor = math.log2(math.e) / math.sqrt(HDIM)
    key_id = lax.broadcasted_iota(jnp.int32, (1, window), 1)

    def cached(j):
        return jnp.concatenate([pool[off_s[j] + b] for b in range(MAXB)], axis=0)

    def attend(items, caches, lens):
        added = [x[rows:] for x in items]
        new_keys = [x.astype(jnp.bfloat16) for x in added]
        new_values = [pltpu.roll(x, steps, 0).astype(jnp.bfloat16) for x in added]
        items = [x[:rows].astype(jnp.bfloat16) for x in items]
        scores, fresh = [], []
        for x, y, cache, size in zip(items, new_keys, caches, lens):
            s = lax.dot_general(
                x, cache()[:, :HDIM], NT, preferred_element_type=jnp.float32
            )
            scores.append(jnp.where(key_id < size * BLK, s, -jnp.inf))
            s = lax.dot_general(x, y, NT, preferred_element_type=jnp.float32)
            fresh.append(s + causal[...])
        tops = [
            jnp.maximum(jnp.max(s, axis=1, keepdims=True), jnp.max(f, axis=1, keepdims=True))
            for s, f in zip(scores, fresh)
        ]
        scores = [jnp.exp2((s - m) * factor) for s, m in zip(scores, tops)]
        fresh = [jnp.exp2((f - m) * factor) for f, m in zip(fresh, tops)]
        results = []
        for y, s, f, cache in zip(new_values, scores, fresh, caches):
            total = jnp.sum(s, axis=1, keepdims=True) + jnp.sum(f, axis=1, keepdims=True)
            o = jnp.dot(
                s.astype(jnp.bfloat16), cache()[:, HDIM:],
                preferred_element_type=jnp.float32,
            )
            o = o + jnp.dot(
                f.astype(jnp.bfloat16), y, preferred_element_type=jnp.float32
            )
            results.append(o / total)
        return results

    def attend_own(items, owners):
        return attend(
            items,
            [functools.partial(cached, j) for j in owners],
            [len_s[me, j] for j in owners],
        )

    def put(i, value):
        res[i] = value

    def stay_group(indices):
        owners = [stay_s[i] for i in indices]
        for i, o in zip(indices, attend_own([item_of(j) for j in owners], owners)):
            put(i, o)

    def move_group(ks):
        owners = [slot_s[k] for k in ks]
        sent = [(used_s[k] > 0) & jnp.logical_not(is_late & (push_k == k)) for k in ks]
        items = [
            jnp.where(ok, q_got[k].astype(jnp.float32), item_of(j))
            for k, j, ok in zip(ks, owners, sent)
        ]
        for k, o in zip(ks, attend_own(items, owners)):
            put(stays + k, o)
            r_out[k] = o.astype(jnp.bfloat16)
        for i in range(len(ks)):
            k = upper * ks[len(ks) - 1 - i] + (1 - upper) * ks[i]

            @pl.when(jnp.logical_not(is_late & (push_k == k)))
            def _():
                send_r(k).start()

    pl.when(meet_at == 0)(meet)
    copy_pool.wait()
    for copy in copy_w:
        copy.start()

    @pl.when(is_late)
    def _():
        push_out[...] = pool[off_s[push_slot] + tp]
        push.start()

    def stay_step(g, carry):
        stay_group([g * group + u for u in range(group)])

        pl.when(meet_at == g + 1)(meet)
        return carry

    lax.fori_loop(0, full, stay_step, 0)
    if stays > full * group:
        stay_group(list(range(full * group, stays)))

    def arrived(count, batch):
        if count > 0:
            got = q_got.at[pl.ds(0, count)]
            pltpu.make_async_copy(got, got, q_recv.at[batch]).wait()

    def serve_near():
        arrived(band - 1, 0)

        def rotation(i):
            other = i + lax.div(i + band - place, band)
            return lax.rem(other - place - 1 + n, n)

        grouped(band - 1, 7, lambda idx: move_group([rotation(i) for i in idx]))

    def far_rotation(i):
        owner = upper * (band - 1 - i) + (1 - upper) * (band + i)
        return lax.rem(owner - me - 1 + n, n)

    def serve_shallow():
        arrived(band - 1, 1)
        grouped(band - 1, 7, lambda idx: move_group([far_rotation(i) for i in idx]))

    def serve_deep():
        pl.when(jnp.logical_not(is_late))(lambda: arrived(1, 2))
        move_group([far_rotation(band - 1)])

    def serve(step):
        if crowded and step == 1:

            @pl.when(upper > 0)
            def _():
                pl.when(jnp.logical_not(is_late))(serve_deep)
                serve_shallow()
                serve_near()

            @pl.when((upper == 0) & jnp.logical_not(is_early))
            def _():
                serve_near()
                serve_shallow()

        elif crowded and step == 2:

            @pl.when(is_early)
            def _():
                serve_near()
                serve_shallow()

            pl.when(upper == 0)(serve_deep)
        elif not crowded and step == 0:
            serve_near()
            serve_shallow()
            serve_deep()

    serve(0)

    def gather(j, carry):
        own_rows = res[pos_s[j]]
        fin[pl.ds(pl.multiple_of(j * rows, 8), rows), :] = jnp.where(
            shift_s[j] > 0, jnp.zeros_like(own_rows), own_rows
        )
        return carry

    lax.fori_loop(0, slots, gather, 0, unroll=8)
    for t in range(steps):
        for h in range(heads):
            lhs[t * slots : (t + 1) * slots, h * HDIM : (h + 1) * HDIM] = fin[
                pl.ds(t * heads + h, slots, stride=rows), :
            ].astype(jnp.bfloat16)
    for c in range(chunks):
        copy_w[c].wait()
    for c in range(chunks):
        o_out[c] = jnp.dot(lhs[...], w_buf[c], preferred_element_type=jnp.float32).astype(
            jnp.bfloat16
        )
    send_o.start()

    serve(1)
    for c in range(chunks):
        copy_w[chunks + c].wait()
    for c in range(chunks):
        main[c] = jnp.dot(lhs[...], w_buf[chunks + c], preferred_element_type=jnp.float32)

    pad = back.shape[0]
    row_id = lax.broadcasted_iota(jnp.int32, (slots, steps * pad), 0)
    col_id = lax.broadcasted_iota(jnp.int32, (slots, steps * pad), 1)
    turns = jnp.zeros((slots, steps * pad), jnp.int32)
    for j in range(slots):
        turns = jnp.where(row_id == j, shift_s[j], turns)
    for t in range(steps):
        spread[t * slots : (t + 1) * slots, :] = jnp.where(
            (turns > 0) & (col_id == turns + (t * pad - 1)), 1.0, 0.0
        ).astype(jnp.bfloat16)

    serve(2)

    @pl.when(is_early)
    def _():
        push.wait_recv()
        relay.start()

    @pl.when(is_early)
    def _():
        relay.wait_recv()
        (o,) = attend(
            [item_of(push_slot)],
            [lambda: jnp.concatenate([push_got[b] for b in range(MAXB)], axis=0)],
            [len_s[mirror, push_slot]],
        )
        r_got[push_k] = o.astype(jnp.bfloat16)

    all_but_one(is_early, r_got, r_recv)
    for k in range(peers, pad):
        back[k] = jnp.zeros((rows, HDIM), jnp.float32)
    for k in range(peers):
        back[k] = r_got[k].astype(jnp.float32)
    flat_back = back.reshape(pad * rows, HDIM)
    for t in range(steps):
        for h in range(heads):
            moved_lhs[t * pad : (t + 1) * pad, h * HDIM : (h + 1) * HDIM] = flat_back[
                pl.ds(t * heads + h, pad, stride=rows), :
            ]
    moved = moved_lhs[...].astype(jnp.bfloat16)
    for c in range(chunks):
        m_out[c] = jnp.dot(moved, w_buf[c], preferred_element_type=jnp.float32).astype(
            jnp.bfloat16
        )
    send_m.start()
    send_o.wait_recv()
    for c in range(chunks):
        own[c] = jnp.dot(moved, w_buf[chunks + c], preferred_element_type=jnp.float32)
        main[c] = main[c] + o_got[c].astype(jnp.float32)
    send_m.wait_recv()
    for c in range(chunks):
        total = (own[c] + m_got[c].astype(jnp.float32)).astype(jnp.bfloat16)
        total = jnp.dot(spread[...], total, preferred_element_type=jnp.float32)
        total = (total + main[c]).astype(out_ref.dtype)
        for t in range(steps):
            out_ref[t, :, c * cols : (c + 1) * cols] = total[t * slots : (t + 1) * slots]
    all_but_one(is_early, q_out, q_send)
    all_but_one(is_late, r_out, r_send)
    send_o.wait_send()
    send_m.wait_send()

    @pl.when(is_late)
    def _():
        push.wait_send()

    @pl.when(is_early)
    def _():
        relay.wait_send()


def body(n, queries, new_kv, cache_pool, lengths, anchor, out_weight):
    steps, slots, width = queries.shape
    features = out_weight.shape[1]
    half = features // lax.axis_size("tp")
    cols = 768 if half % 768 == 0 else half
    chunks = half // cols
    rows = steps * (width // HDIM)
    span = rows + 2 * steps
    peers = n - 1
    pad = -(-peers // 8) * 8
    blocks = cache_pool.shape[0] // BLK
    edge = min(1, n // 4)
    bf16, f32, i32 = jnp.bfloat16, jnp.float32, jnp.int32
    dma = pltpu.SemaphoreType.DMA
    anywhere = pl.BlockSpec(memory_space=pltpu.HBM)
    cache = cache_pool.reshape(blocks, BLK, 2 * HDIM)
    queries, new_kv, cache, lengths, anchor, out_weight = (
        pltpu.with_memory_space_constraint(x, pltpu.HBM)
        for x in (queries, new_kv, cache, lengths, anchor, out_weight)
    )
    return pl.pallas_call(
        functools.partial(kernel, n, edge, cols),
        out_shape=jax.ShapeDtypeStruct((steps, slots, half), bf16),
        in_specs=[anywhere] * 6,
        out_specs=pl.BlockSpec(memory_space=pltpu.VMEM),
        scratch_shapes=[
            pltpu.VMEM(queries.shape, bf16),
            pltpu.VMEM(new_kv.shape, bf16),
            pltpu.VMEM((blocks + MAXB - 1, BLK, 2 * HDIM), bf16),
            pltpu.VMEM((2 * chunks, width, cols), bf16),
            pltpu.VMEM((slots, span, HDIM), f32),
            pltpu.VMEM((slots, rows, HDIM), f32),
            pltpu.VMEM((slots * rows, HDIM), f32),
            pltpu.VMEM((steps * slots, width), bf16),
            pltpu.VMEM((rows, 2 * steps), f32),
            pltpu.VMEM((peers, span, HDIM), bf16),
            pltpu.VMEM((peers, span, HDIM), bf16),
            pltpu.VMEM((peers, rows, HDIM), bf16),
            pltpu.VMEM((peers, rows, HDIM), bf16),
            pltpu.VMEM((chunks, steps * slots, cols), bf16),
            pltpu.VMEM((chunks, steps * slots, cols), bf16),
            pltpu.VMEM((chunks, steps * pad, cols), bf16),
            pltpu.VMEM((chunks, steps * pad, cols), bf16),
            pltpu.VMEM((chunks, steps * slots, cols), f32),
            pltpu.VMEM((chunks, steps * pad, cols), f32),
            pltpu.VMEM((pad, rows, HDIM), f32),
            pltpu.VMEM((steps * pad, width), f32),
            pltpu.VMEM((steps * slots, steps * pad), bf16),
            pltpu.VMEM((BLK, 2 * HDIM), bf16),
            pltpu.VMEM((MAXB, BLK, 2 * HDIM), bf16),
        ]
        + [pltpu.SMEM(lengths.shape, i32), pltpu.SMEM(anchor.shape, i32)]
        + [pltpu.SMEM((max(slots, n),), i32)] * 8
        + [dma((5,)), dma((2 * chunks,))]
        + [dma(()), dma((3,)), dma(()), dma(())]
        + [dma((2,)), dma(()), dma(()), dma((3,))],
        compiler_params=pltpu.CompilerParams(
            collective_id=0, has_side_effects=True, vmem_limit_bytes=48 * 1024 * 1024
        ),
    )(queries, new_kv, cache, lengths, anchor, out_weight)


def solution(mesh):
    n = mesh.shape["inst"]
    placed = (
        P(None, ("groups", "inst"), "tp"),
        P(None, ("groups", "inst"), None),
        P(("groups", "inst"), None),
        P("groups", None),
        P("groups", None),
        P("tp", None),
    )
    return jax.shard_map(
        functools.partial(body, n),
        mesh=mesh,
        in_specs=placed,
        out_specs=P(None, ("groups", "inst"), "tp"),
        check_vma=False,
    )
```

```python
import functools
import math

import jax
import jax.numpy as jnp
from jax import lax
from jax.experimental import pallas as pl
from jax.experimental.pallas import tpu as pltpu
from jax.sharding import PartitionSpec as P

HDIM = 128
BLK = 128
MAXB = 2
MESH = pl.DeviceIdType.MESH
NT = (((1,), (1,)), ((), ()))


def grouped(count, unroll, fn):
    full = count // unroll
    if full == 1:
        fn([i for i in range(unroll)])
    elif full > 1:

        def step(g, carry):
            fn([g * unroll + u for u in range(unroll)])
            return carry

        lax.fori_loop(0, full, step, 0)
    rest = list(range(full * unroll, count))
    if rest:
        fn(rest)


def kernel(
    n, edge, cols, q_hbm, kv_hbm, pool_hbm, len_hbm, anc_hbm, w_hbm, out_ref,
    q_in, kv_in, pool, w_buf, item, res, fin, lhs, causal,
    q_out, q_got, r_out, r_got, o_out, o_got, m_out, m_got, main, own, back, moved_lhs, spread,
    push_out, push_got,
    len_s, anc_s, shift_s, off_s, stay_s, nxt_s, slot_s, used_s, free_s, pos_s,
    in_sem, w_sem, q_send, q_recv, r_send, r_recv, x_send, o_recv, m_recv, p_sem,
):
    steps, slots, width = q_in.shape
    heads = width // HDIM
    rows = steps * heads
    span = rows + 2 * steps
    window = MAXB * BLK
    blocks = pool_hbm.shape[0]
    half = out_ref.shape[2]
    chunks = half // cols
    peers = n - 1
    stays = slots - peers
    me = lax.axis_index("inst")
    tp = lax.axis_index("tp")
    crowded = peers <= slots // 4
    mirror = n - 1 - me
    is_early = me < edge
    is_late = mirror < edge
    push_k = 0
    band = n // 2
    upper = lax.div(me, band)
    place = lax.rem(me, band)
    deepest = lax.div(lax.rem(me + n - 1, n) + 2, n)

    def peer(k):
        return {"inst": lax.rem(me + k, n)}

    barrier = pltpu.get_barrier_semaphore()
    for k in range(peers):

        @pl.when(jnp.logical_not(is_late & (push_k == k)))
        def _():
            pl.semaphore_signal(barrier, inc=1, device_id=peer(k + 1), device_id_type=MESH)

    pl.semaphore_signal(barrier, inc=1, device_id={"tp": 1 - tp}, device_id_type=MESH)

    copy_len = pltpu.make_async_copy(len_hbm, len_s, in_sem.at[0])
    copy_anc = pltpu.make_async_copy(anc_hbm, anc_s, in_sem.at[1])
    copy_q = pltpu.make_async_copy(q_hbm, q_in, in_sem.at[2])
    copy_kv = pltpu.make_async_copy(kv_hbm, kv_in, in_sem.at[3])
    copy_pool = pltpu.make_async_copy(pool_hbm, pool.at[pl.ds(0, blocks)], in_sem.at[4])
    copy_len.start()
    copy_anc.start()
    copy_q.start()
    copy_kv.start()
    copy_pool.start()
    copy_w = []
    for c in range(2 * chunks):
        side = (1 - tp) if c < chunks else tp
        column = pl.multiple_of(side * half + (c % chunks) * cols, cols)
        copy_w.append(
            pltpu.make_async_copy(w_hbm.at[:, pl.ds(column, cols)], w_buf.at[c], w_sem.at[c // chunks])
        )

    def scan_slot(j, carry):
        off, found = carry
        turn = me - anc_s[me, j]
        turn = jnp.where(turn < 0, turn + n, turn)
        shift_s[j] = turn
        off_s[j] = off
        found = tuple(jnp.where(turn == k + 1, j, found[k]) for k in range(peers))
        return off + len_s[me, j], found

    copy_len.wait()
    copy_anc.wait()
    _, found = lax.fori_loop(
        0, slots, scan_slot, (jnp.int32(0), tuple(jnp.int32(-1) for _ in range(peers))),
        unroll=8,
    )

    flat = item.reshape(slots * span, HDIM)
    copy_q.wait()
    copy_kv.wait()
    for t in range(steps):
        for h in range(heads):
            flat[pl.ds(t * heads + h, slots, stride=span), :] = q_in[
                t, :, h * HDIM : (h + 1) * HDIM
            ].astype(jnp.float32)
        for part in range(2):
            flat[pl.ds(rows + part * steps + t, slots, stride=span), :] = kv_in[
                t, :, part * HDIM : (part + 1) * HDIM
            ].astype(jnp.float32)

    def item_of(slot):
        return item[slot]

    for k in range(peers):
        q_out[k] = item_of(jnp.maximum(found[k], 0)).astype(jnp.bfloat16)

    def batch_to(k):
        across = lax.rem(lax.div(lax.rem(me + n - 1 - k, n), band) + upper, 2)
        return across * (1 + deepest)

    def send_q(k):
        return pltpu.make_async_remote_copy(
            src_ref=q_out.at[k], dst_ref=q_got.at[k], send_sem=q_send,
            recv_sem=q_recv.at[batch_to(k)], device_id=peer(n - 1 - k), device_id_type=MESH,
        )

    def send_r(k):
        return pltpu.make_async_remote_copy(
            src_ref=r_out.at[k], dst_ref=r_got.at[k], send_sem=r_send,
            recv_sem=r_recv, device_id=peer(k + 1), device_id_type=MESH,
        )

    send_o = pltpu.make_async_remote_copy(
        src_ref=o_out, dst_ref=o_got, send_sem=x_send.at[0],
        recv_sem=o_recv, device_id={"tp": 1 - tp}, device_id_type=MESH,
    )
    send_m = pltpu.make_async_remote_copy(
        src_ref=m_out, dst_ref=m_got, send_sem=x_send.at[1],
        recv_sem=m_recv, device_id={"tp": 1 - tp}, device_id_type=MESH,
    )
    push = pltpu.make_async_remote_copy(
        src_ref=push_out, dst_ref=push_got.at[tp], send_sem=p_sem.at[0],
        recv_sem=p_sem.at[1], device_id={"inst": mirror}, device_id_type=MESH,
    )
    relay = pltpu.make_async_remote_copy(
        src_ref=push_got.at[tp], dst_ref=push_got.at[tp], send_sem=p_sem.at[0],
        recv_sem=p_sem.at[2], device_id={"tp": 1 - tp}, device_id_type=MESH,
    )

    group = 5
    full = stays // group

    def all_but_one(fewer, ref, sem):
        @pl.when(fewer)
        def _():
            if peers > 1:
                part = ref.at[pl.ds(0, peers - 1)]
                pltpu.make_async_copy(part, part, sem).wait()

        @pl.when(jnp.logical_not(fewer))
        def _():
            pltpu.make_async_copy(ref, ref, sem).wait()

    def greet():
        pl.semaphore_wait(barrier, jnp.where(is_early, n - 1, n))

    def send_all_q():
        for k in range(peers):

            @pl.when(jnp.logical_not(is_early & (push_k == k)))
            def _():
                send_q(k).start()

    def meet():
        greet()
        send_all_q()

    meet_at = jnp.where(me == 0, full, jnp.clip((mirror - 1) // 2 * 2 - 2, 0, full))

    for k in range(peers):
        slot_s[k] = jnp.maximum(found[k], 0)
    push_slot = slot_s[push_k]

    def scan_next(i, cur):
        j = slots - 1 - i
        cur = jnp.where(shift_s[j] == 0, j, cur)
        nxt_s[j] = cur
        return cur

    lax.fori_loop(0, slots, scan_next, jnp.int32(slots - 1), unroll=True)

    def scan_stay(i, cur):
        stay_s[i] = cur
        return nxt_s[jnp.minimum(cur + 1, slots - 1)]

    lax.fori_loop(0, slots, scan_stay, nxt_s[0], unroll=True)
    spare = jnp.int32(0)
    for k in range(peers):
        slot_s[k] = jnp.where(found[k] >= 0, found[k], stay_s[stays + spare])
        used_s[k] = jnp.where(found[k] >= 0, 1, 0)
        spare = spare + jnp.where(found[k] >= 0, 0, 1)
    nxt = jnp.int32(peers - 1)
    for k in reversed(range(peers)):
        nxt = jnp.where(found[k] >= 0, nxt, k)
        nxt_s[k] = nxt
    nxt = nxt_s[0]
    for k in range(peers):
        free_s[k] = nxt
        nxt = nxt_s[jnp.minimum(nxt + 1, peers - 1)]

    def scan_pos(j, count):
        turn = shift_s[j]
        extra = free_s[jnp.clip(count - stays, 0, peers - 1)]
        rest = jnp.where(count < stays, count, stays + extra)
        pos_s[j] = jnp.where(turn > 0, stays + turn - 1, rest)
        return count + jnp.where(turn > 0, 0, 1)

    lax.fori_loop(0, slots, scan_pos, jnp.int32(0), unroll=True)

    pool[blocks] = jnp.zeros((BLK, 2 * HDIM), pool.dtype)
    row_id = lax.broadcasted_iota(jnp.int32, (rows, 2 * steps), 0)
    col_id = lax.broadcasted_iota(jnp.int32, (rows, 2 * steps), 1)
    causal[...] = jnp.where((col_id < steps) & (row_id >= col_id * heads), 0.0, -jnp.inf)

    factor = math.log2(math.e) / math.sqrt(HDIM)
    key_id = lax.broadcasted_iota(jnp.int32, (1, window), 1)

    def cached(j):
        return jnp.concatenate([pool[off_s[j] + b] for b in range(MAXB)], axis=0)

    def attend(items, caches, lens):
        added = [x[rows:] for x in items]
        new_keys = [x.astype(jnp.bfloat16) for x in added]
        new_values = [pltpu.roll(x, steps, 0).astype(jnp.bfloat16) for x in added]
        items = [x[:rows].astype(jnp.bfloat16) for x in items]
        scores, fresh = [], []
        for x, y, cache, size in zip(items, new_keys, caches, lens):
            s = lax.dot_general(
                x, cache()[:, :HDIM], NT, preferred_element_type=jnp.float32
            )
            scores.append(jnp.where(key_id < size * BLK, s, -jnp.inf))
            s = lax.dot_general(x, y, NT, preferred_element_type=jnp.float32)
            fresh.append(s + causal[...])
        tops = [
            jnp.maximum(jnp.max(s, axis=1, keepdims=True), jnp.max(f, axis=1, keepdims=True))
            for s, f in zip(scores, fresh)
        ]
        scores = [jnp.exp2((s - m) * factor) for s, m in zip(scores, tops)]
        fresh = [jnp.exp2((f - m) * factor) for f, m in zip(fresh, tops)]
        results = []
        for y, s, f, cache in zip(new_values, scores, fresh, caches):
            total = jnp.sum(s, axis=1, keepdims=True) + jnp.sum(f, axis=1, keepdims=True)
            o = jnp.dot(
                s.astype(jnp.bfloat16), cache()[:, HDIM:],
                preferred_element_type=jnp.float32,
            )
            o = o + jnp.dot(
                f.astype(jnp.bfloat16), y, preferred_element_type=jnp.float32
            )
            results.append(o / total)
        return results

    def attend_own(items, owners):
        return attend(
            items,
            [functools.partial(cached, j) for j in owners],
            [len_s[me, j] for j in owners],
        )

    def put(i, value):
        res[i] = value

    def stay_group(indices):
        owners = [stay_s[i] for i in indices]
        for i, o in zip(indices, attend_own([item_of(j) for j in owners], owners)):
            put(i, o)

    def move_group(ks):
        owners = [slot_s[k] for k in ks]
        sent = [(used_s[k] > 0) & jnp.logical_not(is_late & (push_k == k)) for k in ks]
        items = [
            jnp.where(ok, q_got[k].astype(jnp.float32), item_of(j))
            for k, j, ok in zip(ks, owners, sent)
        ]
        for k, o in zip(ks, attend_own(items, owners)):
            put(stays + k, o)
            r_out[k] = o.astype(jnp.bfloat16)
        for i in range(len(ks)):
            k = upper * ks[len(ks) - 1 - i] + (1 - upper) * ks[i]

            @pl.when(jnp.logical_not(is_late & (push_k == k)))
            def _():
                send_r(k).start()

    pl.when(meet_at == 0)(meet)
    copy_pool.wait()
    for copy in copy_w:
        copy.start()

    @pl.when(is_late)
    def _():
        push_out[...] = pool[off_s[push_slot] + tp]
        push.start()

    def stay_step(g, carry):
        stay_group([g * group + u for u in range(group)])

        pl.when(meet_at == g + 1)(meet)
        return carry

    lax.fori_loop(0, full, stay_step, 0)
    if stays > full * group:
        stay_group(list(range(full * group, stays)))

    def arrived(count, batch):
        if count > 0:
            got = q_got.at[pl.ds(0, count)]
            pltpu.make_async_copy(got, got, q_recv.at[batch]).wait()

    def serve_near():
        arrived(band - 1, 0)

        def rotation(i):
            other = i + lax.div(i + band - place, band)
            return lax.rem(other - place - 1 + n, n)

        grouped(band - 1, 7, lambda idx: move_group([rotation(i) for i in idx]))

    def far_rotation(i):
        owner = upper * (band - 1 - i) + (1 - upper) * (band + i)
        return lax.rem(owner - me - 1 + n, n)

    def serve_shallow():
        arrived(band - 1, 1)
        grouped(band - 1, 7, lambda idx: move_group([far_rotation(i) for i in idx]))

    def serve_deep():
        pl.when(jnp.logical_not(is_late))(lambda: arrived(1, 2))
        move_group([far_rotation(band - 1)])

    def serve(step):
        if crowded and step == 1:

            @pl.when(upper > 0)
            def _():
                pl.when(jnp.logical_not(is_late))(serve_deep)
                serve_shallow()
                serve_near()

            @pl.when((upper == 0) & jnp.logical_not(is_early))
            def _():
                serve_near()
                serve_shallow()

        elif crowded and step == 2:

            @pl.when(is_early)
            def _():
                serve_near()
                serve_shallow()

            pl.when(upper == 0)(serve_deep)
        elif not crowded and step == 0:
            serve_near()
            serve_shallow()
            serve_deep()

    serve(0)

    def gather(j, carry):
        own_rows = res[pos_s[j]]
        fin[pl.ds(pl.multiple_of(j * rows, 8), rows), :] = jnp.where(
            shift_s[j] > 0, jnp.zeros_like(own_rows), own_rows
        )
        return carry

    lax.fori_loop(0, slots, gather, 0, unroll=8)
    for t in range(steps):
        for h in range(heads):
            lhs[t * slots : (t + 1) * slots, h * HDIM : (h + 1) * HDIM] = fin[
                pl.ds(t * heads + h, slots, stride=rows), :
            ].astype(jnp.bfloat16)
    weights = w_buf.at[pl.ds(0, chunks)]
    pltpu.make_async_copy(weights, weights, w_sem.at[0]).wait()
    for c in range(chunks):
        o_out[c] = jnp.dot(lhs[...], w_buf[c], preferred_element_type=jnp.float32).astype(
            jnp.bfloat16
        )
    send_o.start()

    serve(1)
    weights = w_buf.at[pl.ds(chunks, chunks)]
    pltpu.make_async_copy(weights, weights, w_sem.at[1]).wait()
    for c in range(chunks):
        main[c] = jnp.dot(lhs[...], w_buf[chunks + c], preferred_element_type=jnp.float32)

    pad = back.shape[0]
    row_id = lax.broadcasted_iota(jnp.int32, (slots, steps * pad), 0)
    col_id = lax.broadcasted_iota(jnp.int32, (slots, steps * pad), 1)
    turns = jnp.zeros((slots, steps * pad), jnp.int32)
    for j in range(slots):
        turns = jnp.where(row_id == j, shift_s[j], turns)
    for t in range(steps):
        spread[t * slots : (t + 1) * slots, :] = jnp.where(
            (turns > 0) & (col_id == turns + (t * pad - 1)), 1.0, 0.0
        ).astype(jnp.bfloat16)

    serve(2)

    @pl.when(is_early)
    def _():
        push.wait_recv()
        relay.start()

    @pl.when(is_early)
    def _():
        relay.wait_recv()
        (o,) = attend(
            [item_of(push_slot)],
            [lambda: jnp.concatenate([push_got[b] for b in range(MAXB)], axis=0)],
            [len_s[mirror, push_slot]],
        )
        r_got[push_k] = o.astype(jnp.bfloat16)

    all_but_one(is_early, r_got, r_recv)
    for k in range(peers, pad):
        back[k] = jnp.zeros((rows, HDIM), jnp.float32)
    for k in range(peers):
        back[k] = r_got[k].astype(jnp.float32)
    flat_back = back.reshape(pad * rows, HDIM)
    for t in range(steps):
        for h in range(heads):
            moved_lhs[t * pad : (t + 1) * pad, h * HDIM : (h + 1) * HDIM] = flat_back[
                pl.ds(t * heads + h, pad, stride=rows), :
            ]
    moved = moved_lhs[...].astype(jnp.bfloat16)
    for c in range(chunks):
        m_out[c] = jnp.dot(moved, w_buf[c], preferred_element_type=jnp.float32).astype(
            jnp.bfloat16
        )
    send_m.start()
    send_o.wait_recv()
    for c in range(chunks):
        own[c] = jnp.dot(moved, w_buf[chunks + c], preferred_element_type=jnp.float32)
        main[c] = main[c] + o_got[c].astype(jnp.float32)
    send_m.wait_recv()
    for c in range(chunks):
        total = (own[c] + m_got[c].astype(jnp.float32)).astype(jnp.bfloat16)
        total = jnp.dot(spread[...], total, preferred_element_type=jnp.float32)
        total = (total + main[c]).astype(out_ref.dtype)
        for t in range(steps):
            out_ref[t, :, c * cols : (c + 1) * cols] = total[t * slots : (t + 1) * slots]
    all_but_one(is_early, q_out, q_send)
    all_but_one(is_late, r_out, r_send)
    send_o.wait_send()
    send_m.wait_send()

    @pl.when(is_late)
    def _():
        push.wait_send()

    @pl.when(is_early)
    def _():
        relay.wait_send()


def body(n, queries, new_kv, cache_pool, lengths, anchor, out_weight):
    steps, slots, width = queries.shape
    features = out_weight.shape[1]
    half = features // lax.axis_size("tp")
    cols = 768 if half % 768 == 0 else half
    chunks = half // cols
    rows = steps * (width // HDIM)
    span = rows + 2 * steps
    peers = n - 1
    pad = -(-peers // 8) * 8
    blocks = cache_pool.shape[0] // BLK
    edge = min(1, n // 4)
    bf16, f32, i32 = jnp.bfloat16, jnp.float32, jnp.int32
    dma = pltpu.SemaphoreType.DMA
    anywhere = pl.BlockSpec(memory_space=pltpu.HBM)
    cache = cache_pool.reshape(blocks, BLK, 2 * HDIM)
    queries, new_kv, cache, lengths, anchor, out_weight = (
        pltpu.with_memory_space_constraint(x, pltpu.HBM)
        for x in (queries, new_kv, cache, lengths, anchor, out_weight)
    )
    return pl.pallas_call(
        functools.partial(kernel, n, edge, cols),
        out_shape=jax.ShapeDtypeStruct((steps, slots, half), bf16),
        in_specs=[anywhere] * 6,
        out_specs=pl.BlockSpec(memory_space=pltpu.VMEM),
        scratch_shapes=[
            pltpu.VMEM(queries.shape, bf16),
            pltpu.VMEM(new_kv.shape, bf16),
            pltpu.VMEM((blocks + MAXB - 1, BLK, 2 * HDIM), bf16),
            pltpu.VMEM((2 * chunks, width, cols), bf16),
            pltpu.VMEM((slots, span, HDIM), f32),
            pltpu.VMEM((slots, rows, HDIM), f32),
            pltpu.VMEM((slots * rows, HDIM), f32),
            pltpu.VMEM((steps * slots, width), bf16),
            pltpu.VMEM((rows, 2 * steps), f32),
            pltpu.VMEM((peers, span, HDIM), bf16),
            pltpu.VMEM((peers, span, HDIM), bf16),
            pltpu.VMEM((peers, rows, HDIM), bf16),
            pltpu.VMEM((peers, rows, HDIM), bf16),
            pltpu.VMEM((chunks, steps * slots, cols), bf16),
            pltpu.VMEM((chunks, steps * slots, cols), bf16),
            pltpu.VMEM((chunks, steps * pad, cols), bf16),
            pltpu.VMEM((chunks, steps * pad, cols), bf16),
            pltpu.VMEM((chunks, steps * slots, cols), f32),
            pltpu.VMEM((chunks, steps * pad, cols), f32),
            pltpu.VMEM((pad, rows, HDIM), f32),
            pltpu.VMEM((steps * pad, width), f32),
            pltpu.VMEM((steps * slots, steps * pad), bf16),
            pltpu.VMEM((BLK, 2 * HDIM), bf16),
            pltpu.VMEM((MAXB, BLK, 2 * HDIM), bf16),
        ]
        + [pltpu.SMEM(lengths.shape, i32), pltpu.SMEM(anchor.shape, i32)]
        + [pltpu.SMEM((max(slots, n),), i32)] * 8
        + [dma((5,)), dma((2,))]
        + [dma(()), dma((3,)), dma(()), dma(())]
        + [dma((2,)), dma(()), dma(()), dma((3,))],
        compiler_params=pltpu.CompilerParams(
            collective_id=0, has_side_effects=True, vmem_limit_bytes=48 * 1024 * 1024
        ),
    )(queries, new_kv, cache, lengths, anchor, out_weight)


def solution(mesh):
    n = mesh.shape["inst"]
    placed = (
        P(None, ("groups", "inst"), "tp"),
        P(None, ("groups", "inst"), None),
        P(("groups", "inst"), None),
        P("groups", None),
        P("groups", None),
        P("tp", None),
    )
    return jax.shard_map(
        functools.partial(body, n),
        mesh=mesh,
        in_specs=placed,
        out_specs=P(None, ("groups", "inst"), "tp"),
        check_vma=False,
    )
```
